256 devices in a mesh: segment: 8 (over y, x_hi), lon: 32 (over z, x_lo, core).
Axes of the slice: x: 4 (x_hi: 2, x_lo: 2; x = x_hi * 2 + x_lo), y: 4, z: 8, core: 2. Of those that a mesh axis runs over, the one named last changes fastest.
Arguments:
- patches: bfloat16 [8, 1, 256, 640], P(None, None, 'lon'), may hold values from -4 to 4
- encoder_weight: bfloat16 [640, 1024], replicated, may hold values from -4 to 4
- layer_weights: bfloat16 [8, 4, 1024, 1024], P('segment'), may hold values from -0.1875 to 0.1875
- layer_gains: float32 [8, 1024], P('segment'), may hold values from 0.25 to 1.75
- final_gain: float32 [1024], replicated, may hold values from 0.25 to 1.75
- decoder_weight: bfloat16 [1024, 640], replicated, may hold values from -0.1875 to 0.1875
Outputs:
- forecast: float32 [8, 1, 256, 640], P('segment', None, 'lon')
The draws below stay inside these ranges and needn't reach their ends.
All inputs are finite; a program needn't handle non-finite values.
Results may differ from the reference program's by a relative error of at most 0.015.
Values may be sent and summed in bfloat16 or wider, within the bound.
A program may use at most 64 MiB of HBM per device.

```python
import math
import jax
import jax.numpy as jnp
from jax import lax

WIDTH = 1024
HEADS = 16
HEAD_DIM = 64
PATCH_VALUES = 640
BAND = 1
BANDS = 8
LAYERS = 8
LON = 256


def draw_patches(key, part):
    value_key, scale_key = jax.random.split(key, 2)
    shape_all = (BANDS, BAND, LON, PATCH_VALUES)
    shape_rows = (BANDS, BAND, LON, 1)
    values = jnp.clip(jax.random.normal(value_key, shape_all, jnp.float32), -4.0, 4.0)
    scales = jnp.exp(jax.random.uniform(scale_key, shape_rows, jnp.float32, math.log(0.1), math.log(1.0)))
    return (values * scales).astype(jnp.bfloat16)


def draw_encoder_weight(key, part):
    value_key, scale_key = jax.random.split(key)
    shape_all = (PATCH_VALUES, WIDTH)
    values = jnp.clip(jax.random.normal(value_key, shape_all, jnp.float32), -4.0, 4.0)
    scales = jnp.exp(jax.random.uniform(scale_key, (1, WIDTH), jnp.float32, math.log(0.3), math.log(3.0)))
    return (values * scales * PATCH_VALUES ** (-0.5)).astype(jnp.bfloat16)


def block_levels(own_key, shape, pieces, low, high):
    level, own = 1.0, jax.random.fold_in(own_key, 6)
    for dim, blocks in pieces:
        heights = jnp.exp(jax.random.uniform(jax.random.fold_in(own, dim), (blocks,), jnp.float32, low / len(pieces), high / len(pieces)))
        level = level * jnp.repeat(heights, shape[dim] // blocks).reshape([-1 if axis == dim else 1 for axis in range(len(shape))])
    return level


def centred(rng, shape, spread, most, cuts=(), kind=jnp.bfloat16):
    level = block_levels(rng, shape, cuts, -0.22, 0.18) if cuts else 1.0
    array = jax.random.normal(rng, shape, jnp.float32) * spread * level
    return jnp.minimum(jnp.maximum(array, -most), most).astype(kind)


def setup_inputs(seed: int = 0) -> dict:
    key_list = jax.random.split(jax.random.key(seed), 7)
    return {
        "patches": draw_patches(jax.random.fold_in(key_list[6], 71), 0),
        "encoder_weight": draw_encoder_weight(jax.random.fold_in(key_list[6], 71), 0),
        "layer_weights": centred(key_list[2], (LAYERS, 4, WIDTH, WIDTH), WIDTH ** -0.5, 0.1875, ((0, 8),)),
        "layer_gains": jnp.clip(1.0 + 0.15 * jax.random.normal(key_list[3], (LAYERS, WIDTH), jnp.float32), 0.25, 1.75),
        "final_gain": jnp.clip(1.0 + 0.15 * jax.random.normal(key_list[4], (WIDTH,), jnp.float32), 0.25, 1.75),
        "decoder_weight": centred(key_list[5], (WIDTH, PATCH_VALUES), WIDTH ** -0.5, 0.1875),
    }


SOFTCAP = 5.0
EPSILON = 1e-06

def norm_rows(latent, gain):
    square = lax.optimization_barrier(jnp.mean(latent * latent, axis=-1, keepdims=True))
    return latent * lax.rsqrt(square + EPSILON) * gain

def attention_layer(latent, weights_layer, gain_layer):
    normed = norm_rows(latent.astype(jnp.float32), gain_layer).astype(jnp.bfloat16)
    flat = normed.reshape(-1, WIDTH)
    queries = jnp.dot(flat, weights_layer[0], preferred_element_type=jnp.float32).astype(jnp.bfloat16)
    keys_all = jnp.dot(flat, weights_layer[1], preferred_element_type=jnp.float32).astype(jnp.bfloat16)
    values_all = jnp.dot(flat, weights_layer[2], preferred_element_type=jnp.float32).astype(jnp.bfloat16)
    queries = queries.reshape(BAND, LON, HEADS, HEAD_DIM).astype(jnp.float32)
    keys_all = keys_all.reshape(BAND, LON, HEADS, HEAD_DIM).astype(jnp.float32)
    values_all = values_all.reshape(BAND, LON, HEADS, HEAD_DIM).astype(jnp.float32)
    scores = jnp.einsum('blhe,bmhe->bhlm', queries, keys_all) * HEAD_DIM ** (-0.5)
    capped = SOFTCAP * jnp.tanh(scores / SOFTCAP)
    raised = jnp.exp(capped)
    probability = (raised / lax.optimization_barrier(jnp.sum(raised, axis=-1, keepdims=True))).astype(jnp.bfloat16)
    attended = jnp.einsum('bhlm,bmhe->blhe', probability.astype(jnp.float32), values_all)
    attended = attended.astype(jnp.bfloat16).reshape(-1, WIDTH)
    mixed = latent.astype(jnp.float32).reshape(-1, WIDTH) + jnp.dot(attended, weights_layer[3], preferred_element_type=jnp.float32)
    return mixed.astype(jnp.bfloat16).reshape(BAND, LON, WIDTH)

def reference(patches, encoder_weight, layer_weights, layer_gains, final_gain, decoder_weight):
    results = []
    for band_index in range(BANDS):
        flat = patches[band_index].reshape(-1, PATCH_VALUES)
        latent = jnp.dot(flat, encoder_weight, preferred_element_type=jnp.float32).astype(jnp.bfloat16)
        latent = latent.reshape(BAND, LON, WIDTH)
        for layer_index in range(LAYERS):
            latent = attention_layer(latent, layer_weights[layer_index], layer_gains[layer_index])
        final = norm_rows(latent.astype(jnp.float32), final_gain).astype(jnp.bfloat16).reshape(-1, WIDTH)
        decoded = jnp.dot(final, decoder_weight, preferred_element_type=jnp.float32)
        results.append(decoded.reshape(BAND, LON, PATCH_VALUES))
    return jnp.stack(results)
```

```python
import functools
import math

import jax
import jax.numpy as jnp
from jax import lax
from jax.experimental import pallas as pl
from jax.experimental.pallas import tpu as pltpu
from jax.sharding import PartitionSpec as P

HEAD = 64
SOFTCAP = 5.0
EPSILON = 1e-06
MESH = pl.DeviceIdType.MESH
F32 = jnp.float32
BF16 = jnp.bfloat16


def kernel(
    dims,
    patches,
    encoder_weight,
    layer_weights,
    gain,
    final_gain,
    decoder_weight,
    out,
    pin,
    enc,
    wts,
    dec,
    lat,
    nrm,
    qb,
    kb,
    vb,
    att,
    outl,
    outf,
    fin,
    w_sem,
    in_send,
    in_recv,
    hop_send,
    hop_recv,
    fwd_send,
    fin_send,
    fin_recv,
):
    segs, lons = dims
    nz = lons // 4
    rows_own = patches.shape[1]
    rows = lat.shape[0]
    width = lat.shape[1]
    half = rows // 2
    nq = 2
    qrows = half // nq
    tile = min(256, width)
    s = lax.axis_index("segment")
    lon = lax.axis_index("lon")
    z, xlo, core = lon // 4, lax.rem(lon // 2, 2), lax.rem(lon, 2)
    first, last = s == 0, s == segs - 1
    compute = core == 0
    mine = lax.rem(xlo + s, 2)
    pair = z * 4 + (1 - xlo) * 2

    barrier = pltpu.get_barrier_semaphore()

    def greet(seg, lon_id):
        pl.semaphore_signal(barrier, inc=1, device_id=(seg, lon_id), device_id_type=MESH)

    @pl.when(compute & first)
    def _():
        @pl.loop(0, lons)
        def _(i):
            @pl.when(i != lon)
            def _():
                greet(0, i)

    @pl.when(compute & jnp.logical_not(first))
    def _():
        greet(s - 1, pair)
        greet(s, pair)

    fin_lon = s * 4 + xlo * 2
    fin_self = last & (fin_lon == lon)

    @pl.when(jnp.logical_not(fin_self))
    def _():
        greet(segs - 1, fin_lon)

    def w_copy(i):
        return pltpu.make_async_copy(layer_weights.at[i], wts.at[i], w_sem.at[i])

    enc_copy = pltpu.make_async_copy(encoder_weight, enc, w_sem.at[4])
    dec_copy = pltpu.make_async_copy(decoder_weight, dec, w_sem.at[5])

    @pl.when(compute & first)
    def _():
        enc_copy.start()

    @pl.when(compute)
    def _():
        for i in range(4):
            w_copy(i).start()

    dec_copy.start()

    def count(flag, number):
        return jnp.where(flag, number, 0)

    targets = (
        count(first, 2 * nz)
        - count(first & compute, 1)
        + count(compute & jnp.logical_not(last), 1)
        + count(compute & jnp.logical_not(first), 1)
        + count(compute & last, 2 * nz)
        - count(compute & fin_self, 1)
    )

    @pl.when(targets > 0)
    def _():
        pl.semaphore_wait(barrier, targets)

    slot = (1 - xlo) * (2 * nz) + z * 2 + core

    def in_copy(b, h):
        return pltpu.make_async_remote_copy(
            src_ref=patches.at[b],
            dst_ref=pin.at[slot],
            send_sem=in_send.at[b * 2 + h],
            recv_sem=in_recv.at[slot],
            device_id=(0, b * 4 + h * 2),
            device_id_type=MESH,
        )

    def in_local(b):
        return pltpu.make_async_copy(patches.at[b], pin.at[slot], in_recv.at[slot])

    @pl.when(first)
    def _():
        @pl.loop(0, nz)
        def _(d):
            b = lax.rem(z + nz // 2 + d, nz)
            for h in range(2):
                @pl.when(b * 4 + h * 2 != lon)
                def _():
                    in_copy(b, h).start()

        @pl.when(compute)
        def _():
            in_local(z).start()

    lane = lax.broadcasted_iota(jnp.int32, (1, 128), 1)
    low = lane < HEAD

    @pl.when(compute)
    def _():
        @pl.when(first)
        def _():
            @pl.loop(0, 4 * nz)
            def _(j):
                pltpu.make_async_copy(patches.at[0], pin.at[j], in_recv.at[j]).wait()

            enc_copy.wait()

            @pl.loop(0, width // tile)
            def _(n):
                cols = pl.ds(pl.multiple_of(n * tile, tile), tile)
                flat = pin[...].reshape(rows, pin.shape[2])
                lat[:, cols] = jnp.dot(flat, enc[:, cols], preferred_element_type=F32).astype(BF16)

        for step in range(2):
            part = mine if step == 0 else 1 - mine
            base = part * half

            @pl.when(jnp.logical_not(first))
            def _():
                for k in range(4):
                    chunk = pl.ds(pl.multiple_of(base + k * (half // 4), half // 4), half // 4)
                    copy = pltpu.make_async_remote_copy(
                        src_ref=lat.at[chunk],
                        dst_ref=lat.at[chunk],
                        send_sem=fwd_send.at[k],
                        recv_sem=hop_recv.at[part * 4 + k],
                        device_id=(s, pair),
                        device_id_type=MESH,
                    )
                    copy.wait_recv()
                    if step == 0:
                        copy.start()

            @pl.loop(0, half // 16)
            def _(r):
                sl = pl.ds(pl.multiple_of(base + r * 16, 16), 16)
                x = lat[sl, :].astype(F32)
                square = jnp.mean(x * x, axis=-1, keepdims=True)
                nrm[sl, :] = (x * lax.rsqrt(square + EPSILON) * gain[...]).astype(BF16)

            sl = pl.ds(pl.multiple_of(base, half), half)
            if step == 0:
                for i in range(3):
                    w_copy(i).wait()

            @pl.loop(0, width // tile)
            def _(n):
                cols = pl.ds(pl.multiple_of(n * tile, tile), tile)
                x = nrm[sl, :]
                kb[sl, cols] = jnp.dot(x, wts[1, :, cols], preferred_element_type=F32).astype(BF16)
                vb[sl, cols] = jnp.dot(x, wts[2, :, cols], preferred_element_type=F32).astype(BF16)
                if step == 0:
                    qb[:, cols] = jnp.dot(x, wts[0, :, cols], preferred_element_type=F32).astype(BF16)

        w_copy(3).wait()

        def hop_copy(k):
            return pltpu.make_async_remote_copy(
                src_ref=outl.at[pl.ds(k * (half // 4), half // 4)],
                dst_ref=lat.at[pl.ds(pl.multiple_of(mine * half + k * (half // 4), half // 4), half // 4)],
                send_sem=hop_send.at[k],
                recv_sem=hop_recv.at[mine * 4 + k],
                device_id=(s + 1, pair),
                device_id_type=MESH,
            )

        def fin_target(j):
            return (j // 2) * 4 + xlo * 2 + lax.rem(j, 2)

        def fin_is_self(j):
            return (z == s) & (fin_target(j) == lon)

        def fin_copy(j):
            return pltpu.make_async_remote_copy(
                src_ref=outf.at[j],
                dst_ref=fin,
                send_sem=fin_send.at[j],
                recv_sem=fin_recv,
                device_id=(z, fin_target(j)),
                device_id_type=MESH,
            )

        for c in range(nq):
            @pl.loop(0, width // 128)
            def _(hp):
                lanes = pl.ds(pl.multiple_of(hp * 128, 128), 128)
                q = qb[pl.ds(c * qrows, qrows), lanes]
                zero = jnp.zeros_like(q)
                qs = jnp.concatenate([jnp.where(low, q, zero), jnp.where(low, zero, q)], axis=0)
                scores = lax.dot_general(
                    qs, kb[:, lanes], (((1,), (1,)), ((), ())), preferred_element_type=F32
                )
                capped = jnp.tanh(scores * (1.0 / (SOFTCAP * math.sqrt(HEAD))))
                raised = jnp.exp2(capped * (SOFTCAP * math.log2(math.e)))
                total = jnp.sum(raised, axis=-1, keepdims=True)
                mixed = jnp.dot(raised.astype(BF16), vb[:, lanes], preferred_element_type=F32)
                mixed = mixed * (1.0 / total)
                att[:, lanes] = jnp.where(low, mixed[:qrows], mixed[qrows:]).astype(BF16)

            @pl.loop(0, width // tile)
            def _(n):
                cols = pl.ds(pl.multiple_of(n * tile, tile), tile)
                y = jnp.dot(att[...], wts[3, :, cols], preferred_element_type=F32)
                before = lat[pl.ds(pl.multiple_of(mine * half + c * qrows, qrows), qrows), cols]
                y = (before.astype(F32) + y).astype(BF16)

                @pl.when(jnp.logical_not(last))
                def _():
                    outl[pl.ds(c * qrows, qrows), cols] = y

                @pl.when(last)
                def _():
                    outf[pl.ds(c * (qrows // 8), qrows // 8), :, cols] = y.reshape(qrows // 8, 8, tile)

            @pl.when(jnp.logical_not(last))
            def _():
                for k in range(c * 4 // nq, (c + 1) * 4 // nq):
                    hop_copy(k).start()

            @pl.when(last)
            def _():
                @pl.loop(c * (qrows // 8), (c + 1) * (qrows // 8))
                def _(j):
                    @pl.when(fin_is_self(j))
                    def _():
                        pltpu.make_async_copy(outf.at[j], fin, fin_recv).start()

                    @pl.when(jnp.logical_not(fin_is_self(j)))
                    def _():
                        fin_copy(j).start()

        @pl.when(jnp.logical_not(first))
        def _():
            for k in range(4):
                pltpu.make_async_remote_copy(
                    src_ref=lat.at[pl.ds(0, half // 4)],
                    dst_ref=lat.at[pl.ds(0, half // 4)],
                    send_sem=fwd_send.at[k],
                    recv_sem=hop_recv.at[k],
                    device_id=(s, pair),
                    device_id_type=MESH,
                ).wait_send()

        @pl.when(jnp.logical_not(last))
        def _():
            for k in range(4):
                hop_copy(k).wait_send()

        @pl.when(last)
        def _():
            @pl.loop(0, half // 8)
            def _(j):
                @pl.when(jnp.logical_not(fin_is_self(j)))
                def _():
                    fin_copy(j).wait_send()

    @pl.when(first)
    def _():
        @pl.loop(0, nz)
        def _(b):
            for h in range(2):
                @pl.when(b * 4 + h * 2 != lon)
                def _():
                    in_copy(b, h).wait_send()

    dec_copy.wait()
    pltpu.make_async_copy(outf.at[0], fin, fin_recv).wait()
    x = fin[...].astype(F32)
    square = jnp.mean(x * x, axis=-1, keepdims=True)
    final = (x * lax.rsqrt(square + EPSILON) * final_gain[...]).astype(BF16)
    out[...] = jnp.dot(final, dec[...], preferred_element_type=F32)


def body(dims, patches, encoder_weight, layer_weights, layer_gains, final_gain, decoder_weight):
    bands, band_rows, own, values = patches.shape
    width = encoder_weight.shape[1]
    out_values = decoder_weight.shape[1]
    segs, lons = dims
    rows = own * lons
    half = rows // 2
    anyspace = pl.BlockSpec(memory_space=pl.ANY)
    vmem = pl.BlockSpec(memory_space=pltpu.VMEM)
    dma = pltpu.SemaphoreType.DMA
    decoded = pl.pallas_call(
        functools.partial(kernel, dims),
        out_shape=jax.ShapeDtypeStruct((own, out_values), F32),
        in_specs=[anyspace, anyspace, anyspace, vmem, vmem, anyspace],
        out_specs=vmem,
        scratch_shapes=[
            pltpu.VMEM((lons, own, values), BF16),
            pltpu.VMEM((values, width), BF16),
            pltpu.VMEM((4, width, width), BF16),
            pltpu.VMEM((width, out_values), BF16),
            pltpu.VMEM((rows, width), BF16),
            pltpu.VMEM((rows, width), BF16),
            pltpu.VMEM((half, width), BF16),
            pltpu.VMEM((rows, width), BF16),
            pltpu.VMEM((rows, width), BF16),
            pltpu.VMEM((half // 2, width), BF16),
            pltpu.VMEM((half, width), BF16),
            pltpu.VMEM((half // 8, 8, width), BF16),
            pltpu.VMEM((8, width), BF16),
            dma((6,)),
            dma((lons // 2,)),
            dma((lons,)),
            dma((4,)),
            dma((8,)),
            dma((4,)),
            dma((half // 8,)),
            dma,
        ],
        compiler_params=pltpu.CompilerParams(collective_id=0, has_side_effects=True),
        name="forecast",
    )(
        patches.reshape(bands, own, values),
        encoder_weight,
        layer_weights.reshape(4, width, width),
        layer_gains.reshape(1, width),
        final_gain.reshape(1, width),
        decoder_weight,
    )
    return decoded.reshape(1, band_rows, own, out_values)


def solution(mesh):
    dims = (mesh.shape["segment"], mesh.shape["lon"])
    in_specs = (
        P(None, None, "lon", None),
        P(),
        P("segment", None, None, None),
        P("segment", None),
        P(),
        P(),
    )
    out_specs = P("segment", None, "lon", None)
    return jax.shard_map(
        functools.partial(body, dims), mesh=mesh, in_specs=in_specs, out_specs=out_specs, check_vma=False
    )
```

```python
import functools
import math

import jax
import jax.numpy as jnp
from jax import lax
from jax.experimental import pallas as pl
from jax.experimental.pallas import tpu as pltpu
from jax.sharding import PartitionSpec as P

HEAD = 64
SOFTCAP = 5.0
EPSILON = 1e-06
MESH = pl.DeviceIdType.MESH
F32 = jnp.float32
BF16 = jnp.bfloat16


def kernel(
    dims,
    patches,
    encoder_weight,
    layer_weights,
    gain,
    final_gain,
    decoder_weight,
    out,
    pin,
    enc,
    wts,
    dec,
    lat,
    nrm,
    qb,
    kb,
    vb,
    att,
    outl,
    fin,
    w_sem,
    in_send,
    in_recv,
    hop_send,
    hop_recv,
    fwd_send,
    fin_send,
    fin_recv,
):
    segs, lons = dims
    nz = lons // 4
    rows_own = patches.shape[1]
    rows = lat.shape[0]
    width = lat.shape[1]
    half = rows // 2
    nq = 2
    qrows = half // nq
    tile = min(256, width)
    pieces = fwd_send.shape[0]
    grain = half // pieces
    s = lax.axis_index("segment")
    lon = lax.axis_index("lon")
    z, xlo, core = lon // 4, lax.rem(lon // 2, 2), lax.rem(lon, 2)
    first, last = s == 0, s == segs - 1
    compute = core == 0
    mine = lax.rem(xlo + s, 2)
    pair = z * 4 + (1 - xlo) * 2

    barrier = pltpu.get_barrier_semaphore()

    def greet(seg, lon_id):
        pl.semaphore_signal(barrier, inc=1, device_id=(seg, lon_id), device_id_type=MESH)

    @pl.when(compute & first)
    def _():
        @pl.loop(0, lons)
        def _(i):
            @pl.when(i != lon)
            def _():
                greet(0, i)

    @pl.when(compute & jnp.logical_not(first))
    def _():
        greet(s - 1, pair)
        greet(s, pair)

    fin_lon = s * 4 + xlo * 2
    fin_self = last & (fin_lon == lon)

    @pl.when(jnp.logical_not(fin_self))
    def _():
        greet(segs - 1, fin_lon)

    def w_copy(i):
        return pltpu.make_async_copy(layer_weights.at[i], wts.at[i], w_sem.at[i])

    enc_copy = pltpu.make_async_copy(encoder_weight, enc, w_sem.at[4])
    dec_copy = pltpu.make_async_copy(decoder_weight, dec, w_sem.at[5])

    @pl.when(compute & first)
    def _():
        enc_copy.start()

    @pl.when(compute)
    def _():
        for i in range(4):
            w_copy(i).start()

    dec_copy.start()

    def count(flag, number):
        return jnp.where(flag, number, 0)

    targets = (
        count(first, 2 * nz)
        - count(first & compute, 1)
        + count(compute & jnp.logical_not(last), 1)
        + count(compute & jnp.logical_not(first), 1)
        + count(compute & last, 2 * nz)
        - count(compute & fin_self, 1)
    )

    @pl.when(targets > 0)
    def _():
        pl.semaphore_wait(barrier, targets)

    def place(e):
        far = nz // 2
        return jnp.where(e >= far, jnp.maximum(2 * (e - far) - 1, 0), jnp.minimum(2 * (far - e), nz - 1))

    def in_slot(b):
        return (1 - xlo) * (2 * nz) + place(lax.rem(z - b + nz, nz)) * 2 + core

    def in_copy(b, h):
        slot = in_slot(b)
        return pltpu.make_async_remote_copy(
            src_ref=patches.at[b],
            dst_ref=pin.at[slot],
            send_sem=in_send.at[b * 2 + h],
            recv_sem=in_recv.at[slot],
            device_id=(0, b * 4 + h * 2),
            device_id_type=MESH,
        )

    def in_local(b):
        slot = in_slot(b)
        return pltpu.make_async_copy(patches.at[b], pin.at[slot], in_recv.at[slot])

    @pl.when(first)
    def _():
        @pl.loop(0, nz)
        def _(d):
            b = lax.rem(z + nz // 2 + d, nz)
            for h in range(2):
                @pl.when(b * 4 + h * 2 != lon)
                def _():
                    in_copy(b, h).start()

        @pl.when(compute)
        def _():
            in_local(z).start()

    lane = lax.broadcasted_iota(jnp.int32, (1, 128), 1)
    low = lane < HEAD

    @pl.when(compute)
    def _():
        @pl.when(first)
        def _():
            @pl.loop(0, 4 * nz)
            def _(j):
                pltpu.make_async_copy(patches.at[0], pin.at[j], in_recv.at[j]).wait()

            enc_copy.wait()

            for n in range(width // tile):
                cols = pl.ds(n * tile, tile)
                flat = pin[...].reshape(rows, pin.shape[2])
                lat[:, cols] = jnp.dot(flat, enc[:, cols], preferred_element_type=F32).astype(BF16)

        for step in range(2):
            part = mine if step == 0 else 1 - mine
            base = part * half

            @pl.when(jnp.logical_not(first))
            def _():
                for k in range(pieces):
                    chunk = pl.ds(pl.multiple_of(base + k * grain, grain), grain)
                    copy = pltpu.make_async_remote_copy(
                        src_ref=lat.at[chunk],
                        dst_ref=lat.at[chunk],
                        send_sem=fwd_send.at[k],
                        recv_sem=hop_recv.at[part * pieces + k],
                        device_id=(s, pair),
                        device_id_type=MESH,
                    )
                    copy.wait_recv()
                    if step == 0:
                        copy.start()

            for r in range(half // 16):
                sl = pl.ds(pl.multiple_of(base + r * 16, 16), 16)
                x = lat[sl, :].astype(F32)
                square = jnp.mean(x * x, axis=-1, keepdims=True)
                nrm[sl, :] = (x * lax.rsqrt(square + EPSILON) * gain[...]).astype(BF16)

            sl = pl.ds(pl.multiple_of(base, half), half)
            if step == 0:
                for i in range(3):
                    w_copy(i).wait()

            for n in range(width // tile):
                cols = pl.ds(n * tile, tile)
                x = nrm[sl, :]
                kb[sl, cols] = jnp.dot(x, wts[1, :, cols], preferred_element_type=F32).astype(BF16)
                vb[sl, cols] = jnp.dot(x, wts[2, :, cols], preferred_element_type=F32).astype(BF16)
                if step == 0:
                    qb[:, cols] = jnp.dot(x, wts[0, :, cols], preferred_element_type=F32).astype(BF16)

        w_copy(3).wait()

        def hop_copy(k):
            return pltpu.make_async_remote_copy(
                src_ref=outl.at[pl.ds(k * grain, grain)],
                dst_ref=lat.at[pl.ds(pl.multiple_of(mine * half + k * grain, grain), grain)],
                send_sem=hop_send.at[k],
                recv_sem=hop_recv.at[mine * pieces + k],
                device_id=(s + 1, pair),
                device_id_type=MESH,
            )

        def fin_target(j):
            at = j // 2
            e = nz // 2 + jnp.where(lax.rem(at, 2) == 1, (at + 1) // 2, -(at // 2))
            return lax.rem(z + e, nz) * 4 + xlo * 2 + lax.rem(j, 2)

        def fin_is_self(j):
            return (z == s) & (fin_target(j) == lon)

        def fin_copy(j):
            return pltpu.make_async_remote_copy(
                src_ref=outl.at[pl.ds(pl.multiple_of(j * 8, 8), 8)],
                dst_ref=fin,
                send_sem=fin_send.at[j],
                recv_sem=fin_recv,
                device_id=(z, fin_target(j)),
                device_id_type=MESH,
            )

        for c in range(nq):
            for hp in range(width // 128):
                lanes = pl.ds(hp * 128, 128)
                q = qb[pl.ds(c * qrows, qrows), lanes]
                zero = jnp.zeros_like(q)
                qs = jnp.concatenate([jnp.where(low, q, zero), jnp.where(low, zero, q)], axis=0)
                scores = lax.dot_general(
                    qs, kb[:, lanes], (((1,), (1,)), ((), ())), preferred_element_type=F32
                )
                capped = jnp.tanh(scores * (1.0 / (SOFTCAP * math.sqrt(HEAD))))
                raised = jnp.exp2(capped * (SOFTCAP * math.log2(math.e)))
                total = jnp.sum(raised, axis=-1, keepdims=True)
                mixed = jnp.dot(raised.astype(BF16), vb[:, lanes], preferred_element_type=F32)
                mixed = mixed * (1.0 / total)
                att[:, lanes] = jnp.where(low, mixed[:qrows], mixed[qrows:]).astype(BF16)

            for n in range(width // tile):
                cols = pl.ds(n * tile, tile)
                y = jnp.dot(att[...], wts[3, :, cols], preferred_element_type=F32)
                before = lat[pl.ds(pl.multiple_of(mine * half + c * qrows, qrows), qrows), cols]
                outl[pl.ds(c * qrows, qrows), cols] = (before.astype(F32) + y).astype(BF16)

            @pl.when(jnp.logical_not(last))
            def _():
                for k in range(c * pieces // nq, (c + 1) * pieces // nq):
                    hop_copy(k).start()

            @pl.when(last)
            def _():
                @pl.loop(c * (qrows // 8), (c + 1) * (qrows // 8))
                def _(j):
                    @pl.when(fin_is_self(j))
                    def _():
                        pltpu.make_async_copy(outl.at[pl.ds(pl.multiple_of(j * 8, 8), 8)], fin, fin_recv).start()

                    @pl.when(jnp.logical_not(fin_is_self(j)))
                    def _():
                        fin_copy(j).start()

        @pl.when(jnp.logical_not(first))
        def _():
            for k in range(pieces):
                pltpu.make_async_remote_copy(
                    src_ref=lat.at[pl.ds(0, grain)],
                    dst_ref=lat.at[pl.ds(0, grain)],
                    send_sem=fwd_send.at[k],
                    recv_sem=hop_recv.at[k],
                    device_id=(s, pair),
                    device_id_type=MESH,
                ).wait_send()

        @pl.when(jnp.logical_not(last))
        def _():
            for k in range(pieces):
                hop_copy(k).wait_send()

        @pl.when(last)
        def _():
            @pl.loop(0, half // 8)
            def _(j):
                @pl.when(jnp.logical_not(fin_is_self(j)))
                def _():
                    fin_copy(j).wait_send()

    @pl.when(first)
    def _():
        @pl.loop(0, nz)
        def _(b):
            for h in range(2):
                @pl.when(b * 4 + h * 2 != lon)
                def _():
                    in_copy(b, h).wait_send()

    dec_copy.wait()
    pltpu.make_async_copy(outl.at[pl.ds(0, 8)], fin, fin_recv).wait()
    x = fin[...].astype(F32)
    square = jnp.mean(x * x, axis=-1, keepdims=True)
    final = (x * lax.rsqrt(square + EPSILON) * final_gain[...]).astype(BF16)
    out[...] = jnp.dot(final, dec[...], preferred_element_type=F32)


def body(dims, patches, encoder_weight, layer_weights, layer_gains, final_gain, decoder_weight):
    bands, band_rows, own, values = patches.shape
    width = encoder_weight.shape[1]
    out_values = decoder_weight.shape[1]
    segs, lons = dims
    rows = own * lons
    half = rows // 2
    pieces = half // 16
    anyspace = pl.BlockSpec(memory_space=pl.ANY)
    vmem = pl.BlockSpec(memory_space=pltpu.VMEM)
    dma = pltpu.SemaphoreType.DMA
    decoded = pl.pallas_call(
        functools.partial(kernel, dims),
        out_shape=jax.ShapeDtypeStruct((own, out_values), F32),
        in_specs=[anyspace, anyspace, anyspace, vmem, vmem, anyspace],
        out_specs=vmem,
        scratch_shapes=[
            pltpu.VMEM((lons, own, values), BF16),
            pltpu.VMEM((values, width), BF16),
            pltpu.VMEM((4, width, width), BF16),
            pltpu.VMEM((width, out_values), BF16),
            pltpu.VMEM((rows, width), BF16),
            pltpu.VMEM((rows, width), BF16),
            pltpu.VMEM((half, width), BF16),
            pltpu.VMEM((rows, width), BF16),
            pltpu.VMEM((rows, width), BF16),
            pltpu.VMEM((half // 2, width), BF16),
            pltpu.VMEM((half, width), BF16),
            pltpu.VMEM((8, width), BF16),
            dma((6,)),
            dma((lons // 2,)),
            dma((lons,)),
            dma((pieces,)),
            dma((2 * pieces,)),
            dma((pieces,)),
            dma((half // 8,)),
            dma,
        ],
        compiler_params=pltpu.CompilerParams(collective_id=0, has_side_effects=True),
        name="forecast",
    )(
        patches.reshape(bands, own, values),
        encoder_weight,
        layer_weights.reshape(4, width, width),
        layer_gains.reshape(1, width),
        final_gain.reshape(1, width),
        decoder_weight,
    )
    return decoded.reshape(1, band_rows, own, out_values)


def solution(mesh):
    dims = (mesh.shape["segment"], mesh.shape["lon"])
    in_specs = (
        P(None, None, "lon", None),
        P(),
        P("segment", None, None, None),
        P("segment", None),
        P(),
        P(),
    )
    out_specs = P("segment", None, "lon", None)
    return jax.shard_map(
        functools.partial(body, dims), mesh=mesh, in_specs=in_specs, out_specs=out_specs, check_vma=False
    )
```

```python
import functools
import math

import jax
import jax.numpy as jnp
from jax import lax
from jax.experimental import pallas as pl
from jax.experimental.pallas import tpu as pltpu
from jax.sharding import PartitionSpec as P

HEAD = 64
SOFTCAP = 5.0
EPSILON = 1e-06
MESH = pl.DeviceIdType.MESH
F32 = jnp.float32
BF16 = jnp.bfloat16


def kernel(
    dims,
    patches,
    encoder_weight,
    layer_weights,
    gain,
    final_gain,
    decoder_weight,
    out,
    pin,
    enc,
    wts,
    dec,
    lat,
    nrm,
    qb,
    kb,
    vb,
    att,
    outl,
    fin,
    w_sem,
    in_send,
    in_recv,
    hop_send,
    hop_recv,
    fwd_send,
    fin_send,
    fin_recv,
):
    segs, lons = dims
    nz = lons // 4
    rows_own = patches.shape[1]
    rows = lat.shape[0]
    width = lat.shape[1]
    half = rows // 2
    nq = 2
    qrows = half // nq
    tile = min(256, width)
    pieces = hop_send.shape[0]
    grain = half // pieces
    s = lax.axis_index("segment")
    lon = lax.axis_index("lon")
    z, xlo, core = lon // 4, lax.rem(lon // 2, 2), lax.rem(lon, 2)
    first, last = s == 0, s == segs - 1
    compute = core == 0
    mine = lax.rem(xlo + s, 2)
    pair = z * 4 + (1 - xlo) * 2
    twin = z * 4 + xlo * 2
    forwarder = jnp.logical_not(compute) & jnp.logical_not(first)

    barrier = pltpu.get_barrier_semaphore()

    def greet(seg, lon_id):
        pl.semaphore_signal(barrier, inc=1, device_id=(seg, lon_id), device_id_type=MESH)

    @pl.when(compute & first)
    def _():
        @pl.loop(0, lons)
        def _(i):
            @pl.when(i != lon)
            def _():
                greet(0, i)

    @pl.when(compute & jnp.logical_not(first))
    def _():
        greet(s, twin + 1)
        greet(s, pair + 1)

    @pl.when(forwarder)
    def _():
        greet(s - 1, pair)

    fin_lon = s * 4 + xlo * 2
    fin_self = last & (fin_lon == lon)

    @pl.when(jnp.logical_not(fin_self))
    def _():
        greet(segs - 1, fin_lon)

    def w_copy(i):
        return pltpu.make_async_copy(layer_weights.at[i], wts.at[i], w_sem.at[i])

    enc_copy = pltpu.make_async_copy(encoder_weight, enc, w_sem.at[4])
    dec_copy = pltpu.make_async_copy(decoder_weight, dec, w_sem.at[5])

    @pl.when(compute & first)
    def _():
        enc_copy.start()

    @pl.when(compute)
    def _():
        for i in range(4):
            w_copy(i).start()

    dec_copy.start()

    def count(flag, number):
        return jnp.where(flag, number, 0)

    targets = (
        count(first, 2 * nz)
        - count(first & compute, 1)
        + count(compute & jnp.logical_not(last), 1)
        + count(forwarder, 2)
        + count(compute & last, 2 * nz)
        - count(compute & fin_self, 1)
    )

    @pl.when(targets > 0)
    def _():
        pl.semaphore_wait(barrier, targets)

    def place(e):
        far = nz // 2
        return jnp.where(e >= far, jnp.maximum(2 * (e - far) - 1, 0), jnp.minimum(2 * (far - e), nz - 1))

    def in_slot(b):
        return (1 - xlo) * (2 * nz) + place(lax.rem(z - b + nz, nz)) * 2 + core

    def in_copy(b, h):
        slot = in_slot(b)
        return pltpu.make_async_remote_copy(
            src_ref=patches.at[b],
            dst_ref=pin.at[slot],
            send_sem=in_send.at[b * 2 + h],
            recv_sem=in_recv.at[slot],
            device_id=(0, b * 4 + h * 2),
            device_id_type=MESH,
        )

    def in_local(b):
        slot = in_slot(b)
        return pltpu.make_async_copy(patches.at[b], pin.at[slot], in_recv.at[slot])

    @pl.when(first)
    def _():
        @pl.loop(0, nz)
        def _(d):
            b = lax.rem(z + nz // 2 + d, nz)
            for h in range(2):
                @pl.when(b * 4 + h * 2 != lon)
                def _():
                    in_copy(b, h).start()

        @pl.when(compute)
        def _():
            in_local(z).start()

    def piece_copy(part, k, sem, to):
        chunk = pl.ds(pl.multiple_of(part * half + k * grain, grain), grain)
        return pltpu.make_async_remote_copy(
            src_ref=lat.at[chunk],
            dst_ref=lat.at[chunk],
            send_sem=fwd_send.at[sem],
            recv_sem=hop_recv.at[part * pieces + k],
            device_id=(s, to),
            device_id_type=MESH,
        )

    @pl.when(forwarder)
    def _():
        @pl.loop(0, pieces)
        def _(k):
            piece_copy(mine, k, k, pair).wait_recv()
            piece_copy(mine, k, k, pair).start()
            piece_copy(mine, k, pieces + k, twin).start()

        @pl.loop(0, pieces)
        def _(k):
            piece_copy(mine, k, k, pair).wait_send()
            piece_copy(mine, k, pieces + k, twin).wait_send()

    lane = lax.broadcasted_iota(jnp.int32, (1, 128), 1)
    low = lane < HEAD

    @pl.when(compute)
    def _():
        @pl.when(first)
        def _():
            @pl.loop(0, 4 * nz)
            def _(j):
                pltpu.make_async_copy(patches.at[0], pin.at[j], in_recv.at[j]).wait()

            enc_copy.wait()

            for n in range(width // tile):
                cols = pl.ds(n * tile, tile)
                flat = pin[...].reshape(rows, pin.shape[2])
                lat[:, cols] = jnp.dot(flat, enc[:, cols], preferred_element_type=F32).astype(BF16)

        for step in range(2):
            part = mine if step == 0 else 1 - mine
            base = part * half

            @pl.when(jnp.logical_not(first))
            def _():
                @pl.loop(0, pieces)
                def _(k):
                    piece_copy(part, k, 0, twin).wait_recv()

            for r in range(half // 16):
                sl = pl.ds(pl.multiple_of(base + r * 16, 16), 16)
                x = lat[sl, :].astype(F32)
                square = jnp.mean(x * x, axis=-1, keepdims=True)
                nrm[sl, :] = (x * lax.rsqrt(square + EPSILON) * gain[...]).astype(BF16)

            sl = pl.ds(pl.multiple_of(base, half), half)
            if step == 0:
                for i in range(3):
                    w_copy(i).wait()

            for n in range(width // tile):
                cols = pl.ds(n * tile, tile)
                x = nrm[sl, :]
                kb[sl, cols] = jnp.dot(x, wts[1, :, cols], preferred_element_type=F32).astype(BF16)
                vb[sl, cols] = jnp.dot(x, wts[2, :, cols], preferred_element_type=F32).astype(BF16)
                if step == 0:
                    qb[:, cols] = jnp.dot(x, wts[0, :, cols], preferred_element_type=F32).astype(BF16)

        w_copy(3).wait()

        def hop_copy(k):
            return pltpu.make_async_remote_copy(
                src_ref=outl.at[pl.ds(k * grain, grain)],
                dst_ref=lat.at[pl.ds(pl.multiple_of(mine * half + k * grain, grain), grain)],
                send_sem=hop_send.at[k],
                recv_sem=hop_recv.at[mine * pieces + k],
                device_id=(s + 1, pair + 1),
                device_id_type=MESH,
            )

        def fin_target(j):
            at = j // 2
            e = nz // 2 + jnp.where(lax.rem(at, 2) == 1, (at + 1) // 2, -(at // 2))
            return lax.rem(z + e, nz) * 4 + xlo * 2 + lax.rem(j, 2)

        def fin_is_self(j):
            return (z == s) & (fin_target(j) == lon)

        def fin_copy(j):
            return pltpu.make_async_remote_copy(
                src_ref=outl.at[pl.ds(pl.multiple_of(j * 8, 8), 8)],
                dst_ref=fin,
                send_sem=fin_send.at[j],
                recv_sem=fin_recv,
                device_id=(z, fin_target(j)),
                device_id_type=MESH,
            )

        for c in range(nq):
            for hp in range(width // 128):
                lanes = pl.ds(hp * 128, 128)
                q = qb[pl.ds(c * qrows, qrows), lanes]
                zero = jnp.zeros_like(q)
                qs = jnp.concatenate([jnp.where(low, q, zero), jnp.where(low, zero, q)], axis=0)
                scores = lax.dot_general(
                    qs, kb[:, lanes], (((1,), (1,)), ((), ())), preferred_element_type=F32
                )
                capped = jnp.tanh(scores * (1.0 / (SOFTCAP * math.sqrt(HEAD))))
                raised = jnp.exp2(capped * (SOFTCAP * math.log2(math.e)))
                total = jnp.sum(raised, axis=-1, keepdims=True)
                mixed = jnp.dot(raised.astype(BF16), vb[:, lanes], preferred_element_type=F32)
                mixed = mixed * (1.0 / total)
                att[:, lanes] = jnp.where(low, mixed[:qrows], mixed[qrows:]).astype(BF16)

            for n in range(width // tile):
                cols = pl.ds(n * tile, tile)
                y = jnp.dot(att[...], wts[3, :, cols], preferred_element_type=F32)
                before = lat[pl.ds(pl.multiple_of(mine * half + c * qrows, qrows), qrows), cols]
                outl[pl.ds(c * qrows, qrows), cols] = (before.astype(F32) + y).astype(BF16)

            @pl.when(jnp.logical_not(last))
            def _():
                for k in range(c * pieces // nq, (c + 1) * pieces // nq):
                    hop_copy(k).start()

            @pl.when(last)
            def _():
                @pl.loop(c * (qrows // 8), (c + 1) * (qrows // 8))
                def _(j):
                    @pl.when(fin_is_self(j))
                    def _():
                        pltpu.make_async_copy(outl.at[pl.ds(pl.multiple_of(j * 8, 8), 8)], fin, fin_recv).start()

                    @pl.when(jnp.logical_not(fin_is_self(j)))
                    def _():
                        fin_copy(j).start()

        @pl.when(jnp.logical_not(last))
        def _():
            for k in range(pieces):
                hop_copy(k).wait_send()

        @pl.when(last)
        def _():
            @pl.loop(0, half // 8)
            def _(j):
                @pl.when(jnp.logical_not(fin_is_self(j)))
                def _():
                    fin_copy(j).wait_send()

    @pl.when(first)
    def _():
        @pl.loop(0, nz)
        def _(b):
            for h in range(2):
                @pl.when(b * 4 + h * 2 != lon)
                def _():
                    in_copy(b, h).wait_send()

    dec_copy.wait()
    pltpu.make_async_copy(outl.at[pl.ds(0, 8)], fin, fin_recv).wait()
    x = fin[...].astype(F32)
    square = jnp.mean(x * x, axis=-1, keepdims=True)
    final = (x * lax.rsqrt(square + EPSILON) * final_gain[...]).astype(BF16)
    out[...] = jnp.dot(final, dec[...], preferred_element_type=F32)


def body(dims, patches, encoder_weight, layer_weights, layer_gains, final_gain, decoder_weight):
    bands, band_rows, own, values = patches.shape
    width = encoder_weight.shape[1]
    out_values = decoder_weight.shape[1]
    segs, lons = dims
    rows = own * lons
    half = rows // 2
    pieces = half // 16
    anyspace = pl.BlockSpec(memory_space=pl.ANY)
    vmem = pl.BlockSpec(memory_space=pltpu.VMEM)
    dma = pltpu.SemaphoreType.DMA
    decoded = pl.pallas_call(
        functools.partial(kernel, dims),
        out_shape=jax.ShapeDtypeStruct((own, out_values), F32),
        in_specs=[anyspace, anyspace, anyspace, vmem, vmem, anyspace],
        out_specs=vmem,
        scratch_shapes=[
            pltpu.VMEM((lons, own, values), BF16),
            pltpu.VMEM((values, width), BF16),
            pltpu.VMEM((4, width, width), BF16),
            pltpu.VMEM((width, out_values), BF16),
            pltpu.VMEM((rows, width), BF16),
            pltpu.VMEM((rows, width), BF16),
            pltpu.VMEM((half, width), BF16),
            pltpu.VMEM((rows, width), BF16),
            pltpu.VMEM((rows, width), BF16),
            pltpu.VMEM((half // 2, width), BF16),
            pltpu.VMEM((half, width), BF16),
            pltpu.VMEM((8, width), BF16),
            dma((6,)),
            dma((lons // 2,)),
            dma((lons,)),
            dma((pieces,)),
            dma((2 * pieces,)),
            dma((2 * pieces,)),
            dma((half // 8,)),
            dma,
        ],
        compiler_params=pltpu.CompilerParams(collective_id=0, has_side_effects=True),
        name="forecast",
    )(
        patches.reshape(bands, own, values),
        encoder_weight,
        layer_weights.reshape(4, width, width),
        layer_gains.reshape(1, width),
        final_gain.reshape(1, width),
        decoder_weight,
    )
    return decoded.reshape(1, band_rows, own, out_values)


def solution(mesh):
    dims = (mesh.shape["segment"], mesh.shape["lon"])
    in_specs = (
        P(None, None, "lon", None),
        P(),
        P("segment", None, None, None),
        P("segment", None),
        P(),
        P(),
    )
    out_specs = P("segment", None, "lon", None)
    return jax.shard_map(
        functools.partial(body, dims), mesh=mesh, in_specs=in_specs, out_specs=out_specs, check_vma=False
    )
```

```python
import functools
import math

import jax
import jax.numpy as jnp
from jax import lax
from jax.experimental import pallas as pl
from jax.experimental.pallas import tpu as pltpu
from jax.sharding import PartitionSpec as P

HEAD = 64
SOFTCAP = 5.0
EPSILON = 1e-06
MESH = pl.DeviceIdType.MESH
F32 = jnp.float32
BF16 = jnp.bfloat16


def kernel(
    dims,
    patches,
    encoder_weight,
    layer_weights,
    layer_gain,
    last_gain,
    decoder_weight,
    out,
    pin,
    enc,
    wts,
    dec,
    gain,
    final_gain,
    lat,
    nrm,
    qb,
    kb,
    vb,
    att,
    outl,
    fin,
    w_sem,
    in_send,
    in_recv,
    hop_send,
    hop_recv,
    fwd_send,
    fin_send,
    fin_recv,
):
    segs, lons = dims
    nz = lons // 4
    rows_own = patches.shape[1]
    rows = lat.shape[0]
    width = lat.shape[1]
    half = rows // 2
    nq = 2
    qrows = half // nq
    tile = min(256, width)
    pieces = hop_send.shape[0]
    grain = half // pieces
    s = lax.axis_index("segment")
    lon = lax.axis_index("lon")
    z, xlo, core = lon // 4, lax.rem(lon // 2, 2), lax.rem(lon, 2)
    first, last = s == 0, s == segs - 1
    compute = core == 0
    mine = lax.rem(xlo + s, 2)
    pair = z * 4 + (1 - xlo) * 2
    twin = z * 4 + xlo * 2
    forwarder = jnp.logical_not(compute) & jnp.logical_not(first)

    barrier = pltpu.get_barrier_semaphore()

    def greet(seg, lon_id):
        pl.semaphore_signal(barrier, inc=1, device_id=(seg, lon_id), device_id_type=MESH)

    @pl.when(compute & first)
    def _():
        @pl.loop(0, lons)
        def _(i):
            @pl.when(i != lon)
            def _():
                greet(0, i)

    @pl.when(compute & jnp.logical_not(first))
    def _():
        greet(s, twin + 1)
        greet(s, pair + 1)

    @pl.when(forwarder)
    def _():
        greet(s - 1, pair)

    fin_lon = s * 4 + xlo * 2
    fin_self = last & (fin_lon == lon)

    @pl.when(jnp.logical_not(fin_self))
    def _():
        greet(segs - 1, fin_lon)

    def w_copy(i):
        return pltpu.make_async_copy(layer_weights.at[i], wts.at[i], w_sem.at[i])

    enc_copy = pltpu.make_async_copy(encoder_weight, enc, w_sem.at[4])
    dec_copy = pltpu.make_async_copy(decoder_weight, dec, w_sem.at[5])
    gain_copy = pltpu.make_async_copy(layer_gain, gain, w_sem.at[6])
    last_copy = pltpu.make_async_copy(last_gain, final_gain, w_sem.at[7])

    @pl.when(compute & first)
    def _():
        enc_copy.start()

    @pl.when(compute)
    def _():
        gain_copy.start()
        for i in range(4):
            w_copy(i).start()

    dec_copy.start()
    last_copy.start()

    def count(flag, number):
        return jnp.where(flag, number, 0)

    targets = (
        count(first, 2 * nz)
        - count(first & compute, 1)
        + count(compute & jnp.logical_not(last), 1)
        + count(forwarder, 2)
        + count(compute & last, 2 * nz)
        - count(compute & fin_self, 1)
    )

    @pl.when(targets > 0)
    def _():
        pl.semaphore_wait(barrier, targets)

    def place(e):
        far = nz // 2
        return jnp.where(e >= far, jnp.maximum(2 * (e - far) - 1, 0), jnp.minimum(2 * (far - e), nz - 1))

    def in_slot(b):
        return (1 - xlo) * (2 * nz) + place(lax.rem(z - b + nz, nz)) * 2 + core

    def in_copy(b, h):
        slot = in_slot(b)
        return pltpu.make_async_remote_copy(
            src_ref=patches.at[b],
            dst_ref=pin.at[slot],
            send_sem=in_send.at[b * 2 + h],
            recv_sem=in_recv.at[slot],
            device_id=(0, b * 4 + h * 2),
            device_id_type=MESH,
        )

    def in_local(b):
        slot = in_slot(b)
        return pltpu.make_async_copy(patches.at[b], pin.at[slot], in_recv.at[slot])

    @pl.when(first)
    def _():
        @pl.loop(0, nz)
        def _(d):
            b = lax.rem(z + nz // 2 + d, nz)
            for h in range(2):
                @pl.when(b * 4 + h * 2 != lon)
                def _():
                    in_copy(b, h).start()

        @pl.when(compute)
        def _():
            in_local(z).start()

    def piece_copy(part, k, sem, to):
        chunk = pl.ds(pl.multiple_of(part * half + k * grain, grain), grain)
        return pltpu.make_async_remote_copy(
            src_ref=lat.at[chunk],
            dst_ref=lat.at[chunk],
            send_sem=fwd_send.at[sem],
            recv_sem=hop_recv.at[part * pieces + k],
            device_id=(s, to),
            device_id_type=MESH,
        )

    @pl.when(forwarder)
    def _():
        @pl.loop(0, pieces)
        def _(k):
            piece_copy(mine, k, k, pair).wait_recv()
            piece_copy(mine, k, k, pair).start()
            piece_copy(mine, k, pieces + k, twin).start()

        @pl.loop(0, pieces)
        def _(k):
            piece_copy(mine, k, k, pair).wait_send()
            piece_copy(mine, k, pieces + k, twin).wait_send()

    lane = lax.broadcasted_iota(jnp.int32, (1, 128), 1)
    low = lane < HEAD

    @pl.when(compute)
    def _():
        @pl.when(first)
        def _():
            @pl.loop(0, 4 * nz)
            def _(j):
                pltpu.make_async_copy(patches.at[0], pin.at[j], in_recv.at[j]).wait()

            enc_copy.wait()

            for n in range(width // tile):
                cols = pl.ds(n * tile, tile)
                flat = pin[...].reshape(rows, pin.shape[2])
                lat[:, cols] = jnp.dot(flat, enc[:, cols], preferred_element_type=F32).astype(BF16)

        for step in range(2):
            part = mine if step == 0 else 1 - mine
            base = part * half

            @pl.when(jnp.logical_not(first))
            def _():
                @pl.loop(0, pieces)
                def _(k):
                    piece_copy(part, k, 0, twin).wait_recv()

            if step == 0:
                gain_copy.wait()
            for r in range(half // 16):
                sl = pl.ds(pl.multiple_of(base + r * 16, 16), 16)
                x = lat[sl, :].astype(F32)
                square = jnp.mean(x * x, axis=-1, keepdims=True)
                nrm[sl, :] = (x * lax.rsqrt(square + EPSILON) * gain[...]).astype(BF16)

            sl = pl.ds(pl.multiple_of(base, half), half)
            if step == 0:
                for i in range(3):
                    w_copy(i).wait()

            for n in range(width // tile):
                cols = pl.ds(n * tile, tile)
                x = nrm[sl, :]
                kb[sl, cols] = jnp.dot(x, wts[1, :, cols], preferred_element_type=F32).astype(BF16)
                vb[sl, cols] = jnp.dot(x, wts[2, :, cols], preferred_element_type=F32).astype(BF16)
                if step == 0:
                    qb[:, cols] = jnp.dot(x, wts[0, :, cols], preferred_element_type=F32).astype(BF16)

        w_copy(3).wait()

        def hop_copy(k):
            return pltpu.make_async_remote_copy(
                src_ref=outl.at[pl.ds(k * grain, grain)],
                dst_ref=lat.at[pl.ds(pl.multiple_of(mine * half + k * grain, grain), grain)],
                send_sem=hop_send.at[k],
                recv_sem=hop_recv.at[mine * pieces + k],
                device_id=(s + 1, pair + 1),
                device_id_type=MESH,
            )

        def fin_target(j):
            at = j // 2
            e = nz // 2 + jnp.where(lax.rem(at, 2) == 1, (at + 1) // 2, -(at // 2))
            return lax.rem(z + e, nz) * 4 + xlo * 2 + lax.rem(j, 2)

        def fin_is_self(j):
            return (z == s) & (fin_target(j) == lon)

        def fin_copy(j):
            return pltpu.make_async_remote_copy(
                src_ref=outl.at[pl.ds(pl.multiple_of(j * 8, 8), 8)],
                dst_ref=fin,
                send_sem=fin_send.at[j],
                recv_sem=fin_recv,
                device_id=(z, fin_target(j)),
                device_id_type=MESH,
            )

        for c in range(nq):
            for hp in range(width // 128):
                lanes = pl.ds(hp * 128, 128)
                q = qb[pl.ds(c * qrows, qrows), lanes]
                zero = jnp.zeros_like(q)
                qs = jnp.concatenate([jnp.where(low, q, zero), jnp.where(low, zero, q)], axis=0)
                scores = lax.dot_general(
                    qs, kb[:, lanes], (((1,), (1,)), ((), ())), preferred_element_type=F32
                )
                capped = jnp.tanh(scores * (1.0 / (SOFTCAP * math.sqrt(HEAD))))
                raised = jnp.exp2(capped * (SOFTCAP * math.log2(math.e)))
                total = jnp.sum(raised, axis=-1, keepdims=True)
                mixed = jnp.dot(raised.astype(BF16), vb[:, lanes], preferred_element_type=F32)
                mixed = mixed * (1.0 / total)
                att[:, lanes] = jnp.where(low, mixed[:qrows], mixed[qrows:]).astype(BF16)

            for n in range(width // tile):
                cols = pl.ds(n * tile, tile)
                y = jnp.dot(att[...], wts[3, :, cols], preferred_element_type=F32)
                before = lat[pl.ds(pl.multiple_of(mine * half + c * qrows, qrows), qrows), cols]
                outl[pl.ds(c * qrows, qrows), cols] = (before.astype(F32) + y).astype(BF16)

            @pl.when(jnp.logical_not(last))
            def _():
                for k in range(c * pieces // nq, (c + 1) * pieces // nq):
                    hop_copy(k).start()

            @pl.when(last)
            def _():
                @pl.loop(c * (qrows // 8), (c + 1) * (qrows // 8))
                def _(j):
                    @pl.when(fin_is_self(j))
                    def _():
                        pltpu.make_async_copy(outl.at[pl.ds(pl.multiple_of(j * 8, 8), 8)], fin, fin_recv).start()

                    @pl.when(jnp.logical_not(fin_is_self(j)))
                    def _():
                        fin_copy(j).start()

        @pl.when(jnp.logical_not(last))
        def _():
            for k in range(pieces):
                hop_copy(k).wait_send()

        @pl.when(last)
        def _():
            @pl.loop(0, half // 8)
            def _(j):
                @pl.when(jnp.logical_not(fin_is_self(j)))
                def _():
                    fin_copy(j).wait_send()

    @pl.when(first)
    def _():
        @pl.loop(0, nz)
        def _(b):
            for h in range(2):
                @pl.when(b * 4 + h * 2 != lon)
                def _():
                    in_copy(b, h).wait_send()

    dec_copy.wait()
    last_copy.wait()
    pltpu.make_async_copy(outl.at[pl.ds(0, 8)], fin, fin_recv).wait()
    x = fin[...].astype(F32)
    square = jnp.mean(x * x, axis=-1, keepdims=True)
    final = (x * lax.rsqrt(square + EPSILON) * final_gain[...]).astype(BF16)
    out[...] = jnp.dot(final, dec[...], preferred_element_type=F32)


def body(dims, patches, encoder_weight, layer_weights, layer_gains, final_gain, decoder_weight):
    bands, band_rows, own, values = patches.shape
    width = encoder_weight.shape[1]
    out_values = decoder_weight.shape[1]
    segs, lons = dims
    rows = own * lons
    half = rows // 2
    pieces = half // 8
    anyspace = pl.BlockSpec(memory_space=pl.ANY)
    vmem = pl.BlockSpec(memory_space=pltpu.VMEM)
    dma = pltpu.SemaphoreType.DMA
    decoded = pl.pallas_call(
        functools.partial(kernel, dims),
        out_shape=pltpu.VMEM((own, out_values), F32),
        in_specs=[anyspace] * 6,
        out_specs=vmem,
        scratch_shapes=[
            pltpu.VMEM((lons, own, values), BF16),
            pltpu.VMEM((values, width), BF16),
            pltpu.VMEM((4, width, width), BF16),
            pltpu.VMEM((width, out_values), BF16),
            pltpu.VMEM((1, width), F32),
            pltpu.VMEM((1, width), F32),
            pltpu.VMEM((rows, width), BF16),
            pltpu.VMEM((rows, width), BF16),
            pltpu.VMEM((half, width), BF16),
            pltpu.VMEM((rows, width), BF16),
            pltpu.VMEM((rows, width), BF16),
            pltpu.VMEM((half // 2, width), BF16),
            pltpu.VMEM((half, width), BF16),
            pltpu.VMEM((8, width), BF16),
            dma((8,)),
            dma((lons // 2,)),
            dma((lons,)),
            dma((pieces,)),
            dma((2 * pieces,)),
            dma((2 * pieces,)),
            dma((half // 8,)),
            dma,
        ],
        compiler_params=pltpu.CompilerParams(collective_id=0, has_side_effects=True),
        name="forecast",
    )(
        patches.reshape(bands, own, values),
        encoder_weight,
        layer_weights.reshape(4, width, width),
        layer_gains.reshape(1, width),
        final_gain.reshape(1, width),
        decoder_weight,
    )
    return decoded.reshape(1, band_rows, own, out_values)


def solution(mesh):
    dims = (mesh.shape["segment"], mesh.shape["lon"])
    in_specs = (
        P(None, None, "lon", None),
        P(),
        P("segment", None, None, None),
        P("segment", None),
        P(),
        P(),
    )
    out_specs = P("segment", None, "lon", None)
    return jax.shard_map(
        functools.partial(body, dims), mesh=mesh, in_specs=in_specs, out_specs=out_specs, check_vma=False
    )
```

```python
import functools
import math

import jax
import jax.numpy as jnp
from jax import lax
from jax.experimental import pallas as pl
from jax.experimental.pallas import tpu as pltpu
from jax.sharding import PartitionSpec as P

HEAD = 64
SOFTCAP = 5.0
EPSILON = 1e-06
MESH = pl.DeviceIdType.MESH
SPLIT = 64
F32 = jnp.float32
BF16 = jnp.bfloat16


def kernel(
    dims,
    patches,
    encoder_weight,
    layer_weights,
    layer_gain,
    last_gain,
    decoder_weight,
    out,
    pin,
    enc,
    wts,
    dec,
    gain,
    final_gain,
    lat,
    nrm,
    qb,
    kb,
    vb,
    att,
    outl,
    fin,
    w_sem,
    in_send,
    in_recv,
    hop_send,
    hop_recv,
    fwd_send,
    fin_send,
    fin_recv,
):
    segs, lons = dims
    nz = lons // 4
    rows_own = patches.shape[1]
    rows = lat.shape[0]
    width = lat.shape[1]
    half = rows // 2
    split = half * SPLIT // 128 // 16 * 16 or 16
    tile = min(256, width)
    pieces = hop_send.shape[0]
    grain = half // pieces
    s = lax.axis_index("segment")
    lon = lax.axis_index("lon")
    z, xlo, core = lon // 4, lax.rem(lon // 2, 2), lax.rem(lon, 2)
    first, last = s == 0, s == segs - 1
    compute = core == 0
    mine = lax.rem(xlo + s, 2)
    pair = z * 4 + (1 - xlo) * 2
    twin = z * 4 + xlo * 2
    forwarder = jnp.logical_not(compute) & jnp.logical_not(first)

    barrier = pltpu.get_barrier_semaphore()

    def greet(seg, lon_id):
        pl.semaphore_signal(barrier, inc=1, device_id=(seg, lon_id), device_id_type=MESH)

    @pl.when(compute & first)
    def _():
        @pl.loop(0, lons)
        def _(i):
            @pl.when(i != lon)
            def _():
                greet(0, i)

    @pl.when(compute & jnp.logical_not(first))
    def _():
        greet(s, twin + 1)
        greet(s, pair + 1)

    @pl.when(forwarder)
    def _():
        greet(s - 1, pair)

    fin_lon = s * 4 + xlo * 2
    fin_self = last & (fin_lon == lon)

    @pl.when(jnp.logical_not(fin_self))
    def _():
        greet(segs - 1, fin_lon)

    def w_copy(i):
        return pltpu.make_async_copy(layer_weights.at[i], wts.at[i], w_sem.at[i])

    enc_copy = pltpu.make_async_copy(encoder_weight, enc, w_sem.at[4])
    dec_copy = pltpu.make_async_copy(decoder_weight, dec, w_sem.at[5])
    gain_copy = pltpu.make_async_copy(layer_gain, gain, w_sem.at[6])
    last_copy = pltpu.make_async_copy(last_gain, final_gain, w_sem.at[7])

    @pl.when(compute & first)
    def _():
        enc_copy.start()

    @pl.when(compute)
    def _():
        gain_copy.start()
        for i in range(4):
            w_copy(i).start()

    dec_copy.start()
    last_copy.start()

    def count(flag, number):
        return jnp.where(flag, number, 0)

    targets = (
        count(first, 2 * nz)
        - count(first & compute, 1)
        + count(compute & jnp.logical_not(last), 1)
        + count(forwarder, 2)
        + count(compute & last, 2 * nz)
        - count(compute & fin_self, 1)
    )

    @pl.when(targets > 0)
    def _():
        pl.semaphore_wait(barrier, targets)

    def place(e):
        far = nz // 2
        return jnp.where(e >= far, jnp.maximum(2 * (e - far) - 1, 0), jnp.minimum(2 * (far - e), nz - 1))

    def offset(at):
        return nz // 2 + jnp.where(lax.rem(at, 2) == 1, (at + 1) // 2, -(at // 2))

    def in_slot(b):
        return (1 - xlo) * (2 * nz) + place(lax.rem(z - b + nz, nz)) * 2 + core

    def in_copy(b, h):
        slot = in_slot(b)
        return pltpu.make_async_remote_copy(
            src_ref=patches.at[b],
            dst_ref=pin.at[slot],
            send_sem=in_send.at[b * 2 + h],
            recv_sem=in_recv.at[slot],
            device_id=(0, b * 4 + h * 2),
            device_id_type=MESH,
        )

    def in_local(b):
        slot = in_slot(b)
        return pltpu.make_async_copy(patches.at[b], pin.at[slot], in_recv.at[slot])

    @pl.when(first)
    def _():
        @pl.loop(0, nz)
        def _(d):
            b = lax.rem(z + offset(nz - 1 - d), nz)
            for h in range(2):
                @pl.when(b * 4 + h * 2 != lon)
                def _():
                    in_copy(b, h).start()

        @pl.when(compute)
        def _():
            in_local(z).start()

    def piece_copy(part, k, sem, to):
        chunk = pl.ds(pl.multiple_of(part * half + k * grain, grain), grain)
        return pltpu.make_async_remote_copy(
            src_ref=lat.at[chunk],
            dst_ref=lat.at[chunk],
            send_sem=fwd_send.at[sem],
            recv_sem=hop_recv.at[part * pieces + k],
            device_id=(s, to),
            device_id_type=MESH,
        )

    @pl.when(forwarder)
    def _():
        @pl.loop(0, pieces)
        def _(k):
            piece_copy(mine, k, k, pair).wait_recv()
            piece_copy(mine, k, k, pair).start()
            piece_copy(mine, k, pieces + k, twin).start()

        @pl.loop(0, pieces)
        def _(k):
            piece_copy(mine, k, k, pair).wait_send()
            piece_copy(mine, k, pieces + k, twin).wait_send()

    lane = lax.broadcasted_iota(jnp.int32, (1, 128), 1)
    low = lane < HEAD

    def normalise(base, many):
        for r in range(many // 16):
            sl = pl.ds(pl.multiple_of(base + r * 16, 16), 16)
            x = lat[sl, :].astype(F32)
            square = jnp.mean(x * x, axis=-1, keepdims=True)
            nrm[sl, :] = (x * lax.rsqrt(square + EPSILON) * gain[...]).astype(BF16)

    def product(x, which, cols):
        return jnp.dot(x, wts[which, :, cols], preferred_element_type=F32).astype(BF16)

    def ready():
        gain_copy.wait()
        for i in range(4):
            w_copy(i).wait()

    def hop_copy(k):
        return pltpu.make_async_remote_copy(
            src_ref=outl.at[pl.ds(k * grain, grain)],
            dst_ref=lat.at[pl.ds(pl.multiple_of(mine * half + k * grain, grain), grain)],
            send_sem=hop_send.at[k],
            recv_sem=hop_recv.at[mine * pieces + k],
            device_id=(s + 1, pair + 1),
            device_id_type=MESH,
        )

    def fin_target(j):
        return lax.rem(z + offset(j // 2), nz) * 4 + xlo * 2 + lax.rem(j, 2)

    def fin_is_self(j):
        return (z == s) & (fin_target(j) == lon)

    def fin_copy(j):
        return pltpu.make_async_remote_copy(
            src_ref=outl.at[pl.ds(pl.multiple_of(j * 8, 8), 8)],
            dst_ref=fin,
            send_sem=fin_send.at[j],
            recv_sem=fin_recv,
            device_id=(z, fin_target(j)),
            device_id_type=MESH,
        )

    def attend_and_send():
        for start, qrows in ((0, split), (split, half - split)):
            for hp in range(width // 128):
                lanes = pl.ds(hp * 128, 128)
                q = qb[pl.ds(start, qrows), lanes]
                zero = jnp.zeros_like(q)
                qs = jnp.concatenate([jnp.where(low, q, zero), jnp.where(low, zero, q)], axis=0)
                scores = lax.dot_general(
                    qs, kb[:, lanes], (((1,), (1,)), ((), ())), preferred_element_type=F32
                )
                capped = jnp.tanh(scores * (1.0 / (SOFTCAP * math.sqrt(HEAD))))
                raised = jnp.exp2(capped * (SOFTCAP * math.log2(math.e)))
                total = jnp.sum(raised, axis=-1, keepdims=True)
                mixed = jnp.dot(raised.astype(BF16), vb[:, lanes], preferred_element_type=F32)
                mixed = mixed * (1.0 / total)
                att[pl.ds(0, qrows), lanes] = jnp.where(low, mixed[:qrows], mixed[qrows:]).astype(BF16)

            for n in range(width // tile):
                cols = pl.ds(n * tile, tile)
                y = jnp.dot(att[pl.ds(0, qrows), :], wts[3, :, cols], preferred_element_type=F32)
                before = lat[pl.ds(pl.multiple_of(mine * half + start, 16), qrows), cols]
                outl[pl.ds(start, qrows), cols] = (before.astype(F32) + y).astype(BF16)

            @pl.when(jnp.logical_not(last))
            def _():
                for k in range(start // grain, (start + qrows) // grain):
                    hop_copy(k).start()

            @pl.when(last)
            def _():
                @pl.loop(start // 8, (start + qrows) // 8)
                def _(j):
                    @pl.when(fin_is_self(j))
                    def _():
                        pltpu.make_async_copy(outl.at[pl.ds(pl.multiple_of(j * 8, 8), 8)], fin, fin_recv).start()

                    @pl.when(jnp.logical_not(fin_is_self(j)))
                    def _():
                        fin_copy(j).start()

    @pl.when(compute & first)
    def _():
        enc_copy.wait()
        block = half // 2
        for begin in (block, 0):
            @pl.loop(0, 2 * nz)
            def _(j):
                at = lax.rem(j, nz) + (j // nz) * (2 * nz) + begin // 8
                pltpu.make_async_copy(patches.at[0], pin.at[at], in_recv.at[at]).wait()

            values = pin.shape[2]
            flat = jnp.concatenate(
                [pin[pl.ds((h * half + begin) // 8, nz)].reshape(block, values) for h in range(2)], axis=0
            )
            for n in range(width // tile):
                cols = pl.ds(n * tile, tile)
                fresh = jnp.dot(flat, enc[:, cols], preferred_element_type=F32).astype(BF16)
                lat[pl.ds(begin, block), cols] = fresh[:block]
                lat[pl.ds(half + begin, block), cols] = fresh[block:]

            if begin:
                ready()

            normalise(begin, block)
            normalise(half + begin, block)
            both = jnp.concatenate([nrm[pl.ds(h * half + begin, block), :] for h in range(2)], axis=0)
            here = nrm[pl.ds(pl.multiple_of(mine * half + begin, block), block), :]
            for n in range(width // tile):
                cols = pl.ds(n * tile, tile)
                keys, vals = product(both, 1, cols), product(both, 2, cols)
                for h in range(2):
                    kb[pl.ds(h * half + begin, block), cols] = keys[h * block : (h + 1) * block]
                    vb[pl.ds(h * half + begin, block), cols] = vals[h * block : (h + 1) * block]
                qb[pl.ds(begin, block), cols] = product(here, 0, cols)

        attend_and_send()

    @pl.when(compute & jnp.logical_not(first))
    def _():
        for step in range(2):
            part = mine if step == 0 else 1 - mine

            @pl.loop(0, pieces)
            def _(k):
                piece_copy(part, k, 0, twin).wait_recv()

            if step == 0:
                ready()
            normalise(part * half, half)
            sl = pl.ds(pl.multiple_of(part * half, half), half)
            for n in range(width // tile):
                cols = pl.ds(n * tile, tile)
                x = nrm[sl, :]
                kb[sl, cols] = product(x, 1, cols)
                vb[sl, cols] = product(x, 2, cols)
                if step == 0:
                    qb[:, cols] = product(x, 0, cols)

        attend_and_send()

    @pl.when(compute)
    def _():
        @pl.when(jnp.logical_not(last))
        def _():
            for k in range(pieces):
                hop_copy(k).wait_send()

        @pl.when(last)
        def _():
            @pl.loop(0, half // 8)
            def _(j):
                @pl.when(jnp.logical_not(fin_is_self(j)))
                def _():
                    fin_copy(j).wait_send()

    @pl.when(first)
    def _():
        @pl.loop(0, nz)
        def _(b):
            for h in range(2):
                @pl.when(b * 4 + h * 2 != lon)
                def _():
                    in_copy(b, h).wait_send()

    dec_copy.wait()
    last_copy.wait()
    pltpu.make_async_copy(outl.at[pl.ds(0, 8)], fin, fin_recv).wait()
    x = fin[...].astype(F32)
    square = jnp.mean(x * x, axis=-1, keepdims=True)
    final = (x * lax.rsqrt(square + EPSILON) * final_gain[...]).astype(BF16)
    out[...] = jnp.dot(final, dec[...], preferred_element_type=F32)


def body(dims, patches, encoder_weight, layer_weights, layer_gains, final_gain, decoder_weight):
    bands, band_rows, own, values = patches.shape
    width = encoder_weight.shape[1]
    out_values = decoder_weight.shape[1]
    segs, lons = dims
    rows = own * lons
    half = rows // 2
    pieces = half // 8
    anyspace = pl.BlockSpec(memory_space=pl.ANY)
    vmem = pl.BlockSpec(memory_space=pltpu.VMEM)
    dma = pltpu.SemaphoreType.DMA
    decoded = pl.pallas_call(
        functools.partial(kernel, dims),
        out_shape=pltpu.VMEM((own, out_values), F32),
        in_specs=[anyspace] * 6,
        out_specs=vmem,
        scratch_shapes=[
            pltpu.VMEM((lons, own, values), BF16),
            pltpu.VMEM((values, width), BF16),
            pltpu.VMEM((4, width, width), BF16),
            pltpu.VMEM((width, out_values), BF16),
            pltpu.VMEM((1, width), F32),
            pltpu.VMEM((1, width), F32),
            pltpu.VMEM((rows, width), BF16),
            pltpu.VMEM((rows, width), BF16),
            pltpu.VMEM((half, width), BF16),
            pltpu.VMEM((rows, width), BF16),
            pltpu.VMEM((rows, width), BF16),
            pltpu.VMEM((half, width), BF16),
            pltpu.VMEM((half, width), BF16),
            pltpu.VMEM((8, width), BF16),
            dma((8,)),
            dma((lons // 2,)),
            dma((lons,)),
            dma((pieces,)),
            dma((2 * pieces,)),
            dma((2 * pieces,)),
            dma((half // 8,)),
            dma,
        ],
        compiler_params=pltpu.CompilerParams(collective_id=0, has_side_effects=True),
        name="forecast",
    )(
        patches.reshape(bands, own, values),
        encoder_weight,
        layer_weights.reshape(4, width, width),
        layer_gains.reshape(1, width),
        final_gain.reshape(1, width),
        decoder_weight,
    )
    return decoded.reshape(1, band_rows, own, out_values)


def solution(mesh):
    dims = (mesh.shape["segment"], mesh.shape["lon"])
    in_specs = (
        P(None, None, "lon", None),
        P(),
        P("segment", None, None, None),
        P("segment", None),
        P(),
        P(),
    )
    out_specs = P("segment", None, "lon", None)
    return jax.shard_map(
        functools.partial(body, dims), mesh=mesh, in_specs=in_specs, out_specs=out_specs, check_vma=False
    )
```

```python
import functools
import math

import jax
import jax.numpy as jnp
from jax import lax
from jax.experimental import pallas as pl
from jax.experimental.pallas import tpu as pltpu
from jax.sharding import PartitionSpec as P

HEAD = 64
SOFTCAP = 5.0
EPSILON = 1e-06
MESH = pl.DeviceIdType.MESH
SPLIT = 64
F32 = jnp.float32
BF16 = jnp.bfloat16


def kernel(
    dims,
    patches,
    encoder_weight,
    layer_weights,
    layer_gain,
    last_gain,
    decoder_weight,
    out,
    pin,
    enc,
    wts,
    dec,
    gain,
    final_gain,
    lat,
    nrm,
    qb,
    kb,
    vb,
    att,
    outl,
    fin,
    w_sem,
    in_send,
    in_recv,
    hop_send,
    hop_recv,
    fwd_send,
    fin_send,
    fin_recv,
):
    segs, lons = dims
    nz = lons // 4
    rows_own = patches.shape[1]
    rows = lat.shape[0]
    width = lat.shape[1]
    half = rows // 2
    split = half * SPLIT // 128 // 16 * 16 or 16
    tile = min(256, width)
    pieces = hop_send.shape[0]
    grain = half // pieces
    s = lax.axis_index("segment")
    lon = lax.axis_index("lon")
    z, xlo, core = lon // 4, lax.rem(lon // 2, 2), lax.rem(lon, 2)
    first, last = s == 0, s == segs - 1
    compute = core == 0
    mine = lax.rem(xlo + s, 2)
    pair = z * 4 + (1 - xlo) * 2
    twin = z * 4 + xlo * 2
    forwarder = jnp.logical_not(compute) & jnp.logical_not(first)

    barrier = pltpu.get_barrier_semaphore()

    def greet(seg, lon_id):
        pl.semaphore_signal(barrier, inc=1, device_id=(seg, lon_id), device_id_type=MESH)

    @pl.when(compute & first)
    def _():
        @pl.loop(0, lons)
        def _(i):
            @pl.when(i != lon)
            def _():
                greet(0, i)

    @pl.when(compute & jnp.logical_not(first))
    def _():
        greet(s, twin + 1)
        greet(s, pair + 1)

    @pl.when(forwarder)
    def _():
        greet(s - 1, pair)

    fin_lon = s * 4 + xlo * 2
    fin_self = last & (fin_lon == lon)

    @pl.when(jnp.logical_not(fin_self))
    def _():
        greet(segs - 1, fin_lon)

    def w_copy(i):
        return pltpu.make_async_copy(layer_weights.at[i], wts.at[i], w_sem.at[i])

    enc_copy = pltpu.make_async_copy(encoder_weight, enc, w_sem.at[4])
    dec_copy = pltpu.make_async_copy(decoder_weight, dec, w_sem.at[5])
    gain_copy = pltpu.make_async_copy(layer_gain, gain, w_sem.at[6])
    last_copy = pltpu.make_async_copy(last_gain, final_gain, w_sem.at[7])

    @pl.when(compute & first)
    def _():
        enc_copy.start()

    @pl.when(compute)
    def _():
        gain_copy.start()
        for i in range(4):
            w_copy(i).start()

    dec_copy.start()
    last_copy.start()

    def count(flag, number):
        return jnp.where(flag, number, 0)

    targets = (
        count(first, 2 * nz)
        - count(first & compute, 1)
        + count(compute & jnp.logical_not(last), 1)
        + count(forwarder, 2)
        + count(compute & last, 2 * nz)
        - count(compute & fin_self, 1)
    )

    @pl.when(targets > 0)
    def _():
        pl.semaphore_wait(barrier, targets)

    def place(e):
        far = nz // 2
        return jnp.where(e >= far, jnp.maximum(2 * (e - far) - 1, 0), jnp.minimum(2 * (far - e), nz - 1))

    def offset(at):
        return nz // 2 + jnp.where(lax.rem(at, 2) == 1, (at + 1) // 2, -(at // 2))

    def in_slot(b):
        return (1 - xlo) * (2 * nz) + place(lax.rem(z - b + nz, nz)) * 2 + core

    def in_copy(b, h):
        slot = in_slot(b)
        return pltpu.make_async_remote_copy(
            src_ref=patches.at[b],
            dst_ref=pin.at[slot],
            send_sem=in_send.at[b * 2 + h],
            recv_sem=in_recv.at[slot],
            device_id=(0, b * 4 + h * 2),
            device_id_type=MESH,
        )

    def in_local(b):
        slot = in_slot(b)
        return pltpu.make_async_copy(patches.at[b], pin.at[slot], in_recv.at[slot])

    @pl.when(first)
    def _():
        @pl.loop(0, nz)
        def _(d):
            b = lax.rem(z + offset(nz - 1 - d), nz)
            for i in range(2):
                h = 1 - xlo if i == 0 else xlo

                @pl.when(b * 4 + h * 2 != lon)
                def _():
                    in_copy(b, h).start()

        @pl.when(compute)
        def _():
            in_local(z).start()

    def piece_copy(part, k, sem, to):
        chunk = pl.ds(pl.multiple_of(part * half + k * grain, grain), grain)
        return pltpu.make_async_remote_copy(
            src_ref=lat.at[chunk],
            dst_ref=lat.at[chunk],
            send_sem=fwd_send.at[sem],
            recv_sem=hop_recv.at[part * pieces + k],
            device_id=(s, to),
            device_id_type=MESH,
        )

    @pl.when(forwarder)
    def _():
        @pl.loop(0, pieces)
        def _(k):
            piece_copy(mine, k, k, pair).wait_recv()
            piece_copy(mine, k, k, pair).start()
            piece_copy(mine, k, pieces + k, twin).start()

        @pl.loop(0, pieces)
        def _(k):
            piece_copy(mine, k, k, pair).wait_send()
            piece_copy(mine, k, pieces + k, twin).wait_send()

    lane = lax.broadcasted_iota(jnp.int32, (1, 128), 1)
    low = lane < HEAD

    def normalise(base, many):
        for r in range(many // 16):
            sl = pl.ds(pl.multiple_of(base + r * 16, 16), 16)
            x = lat[sl, :].astype(F32)
            square = jnp.mean(x * x, axis=-1, keepdims=True)
            nrm[sl, :] = (x * lax.rsqrt(square + EPSILON) * gain[...]).astype(BF16)

    def product(x, which, cols):
        return jnp.dot(x, wts[which, :, cols], preferred_element_type=F32).astype(BF16)

    def ready():
        gain_copy.wait()
        for i in range(4):
            w_copy(i).wait()

    def hop_copy(k):
        return pltpu.make_async_remote_copy(
            src_ref=outl.at[pl.ds(k * grain, grain)],
            dst_ref=lat.at[pl.ds(pl.multiple_of(mine * half + k * grain, grain), grain)],
            send_sem=hop_send.at[k],
            recv_sem=hop_recv.at[mine * pieces + k],
            device_id=(s + 1, pair + 1),
            device_id_type=MESH,
        )

    def fin_target(j):
        return lax.rem(z + offset(j // 2), nz) * 4 + xlo * 2 + lax.rem(j, 2)

    def fin_is_self(j):
        return (z == s) & (fin_target(j) == lon)

    def fin_copy(j):
        return pltpu.make_async_remote_copy(
            src_ref=outl.at[pl.ds(pl.multiple_of(j * 8, 8), 8)],
            dst_ref=fin,
            send_sem=fin_send.at[j],
            recv_sem=fin_recv,
            device_id=(z, fin_target(j)),
            device_id_type=MESH,
        )

    def attend_and_send():
        for start, qrows in ((0, split), (split, half - split)):
            for hp in range(width // 128):
                lanes = pl.ds(hp * 128, 128)
                q = qb[pl.ds(start, qrows), lanes]
                zero = jnp.zeros_like(q)
                qs = jnp.concatenate([jnp.where(low, q, zero), jnp.where(low, zero, q)], axis=0)
                scores = lax.dot_general(
                    qs, kb[:, lanes], (((1,), (1,)), ((), ())), preferred_element_type=F32
                )
                capped = jnp.tanh(scores * (1.0 / (SOFTCAP * math.sqrt(HEAD))))
                raised = jnp.exp2(capped * (SOFTCAP * math.log2(math.e)))
                total = jnp.sum(raised, axis=-1, keepdims=True)
                mixed = jnp.dot(raised.astype(BF16), vb[:, lanes], preferred_element_type=F32)
                mixed = mixed * (1.0 / total)
                att[pl.ds(0, qrows), lanes] = jnp.where(low, mixed[:qrows], mixed[qrows:]).astype(BF16)

            for n in range(width // tile):
                cols = pl.ds(n * tile, tile)
                y = jnp.dot(att[pl.ds(0, qrows), :], wts[3, :, cols], preferred_element_type=F32)
                before = lat[pl.ds(pl.multiple_of(mine * half + start, 16), qrows), cols]
                outl[pl.ds(start, qrows), cols] = (before.astype(F32) + y).astype(BF16)

            @pl.when(jnp.logical_not(last))
            def _():
                for k in range(start // grain, (start + qrows) // grain):
                    hop_copy(k).start()

            @pl.when(last)
            def _():
                @pl.loop(start // 8, (start + qrows) // 8)
                def _(j):
                    @pl.when(fin_is_self(j))
                    def _():
                        pltpu.make_async_copy(outl.at[pl.ds(pl.multiple_of(j * 8, 8), 8)], fin, fin_recv).start()

                    @pl.when(jnp.logical_not(fin_is_self(j)))
                    def _():
                        fin_copy(j).start()

    @pl.when(compute & first)
    def _():
        enc_copy.wait()
        block = half // 2
        for begin in (block, 0):
            @pl.loop(0, 2 * nz)
            def _(j):
                at = lax.rem(j, nz) + (j // nz) * (2 * nz) + begin // 8
                pltpu.make_async_copy(patches.at[0], pin.at[at], in_recv.at[at]).wait()

            values = pin.shape[2]
            flat = jnp.concatenate(
                [pin[pl.ds((h * half + begin) // 8, nz)].reshape(block, values) for h in range(2)], axis=0
            )
            for n in range(width // tile):
                cols = pl.ds(n * tile, tile)
                fresh = jnp.dot(flat, enc[:, cols], preferred_element_type=F32).astype(BF16)
                lat[pl.ds(begin, block), cols] = fresh[:block]
                lat[pl.ds(half + begin, block), cols] = fresh[block:]

            if begin:
                ready()

            normalise(begin, block)
            normalise(half + begin, block)
            both = jnp.concatenate([nrm[pl.ds(h * half + begin, block), :] for h in range(2)], axis=0)
            here = nrm[pl.ds(pl.multiple_of(mine * half + begin, block), block), :]
            for n in range(width // tile):
                cols = pl.ds(n * tile, tile)
                keys, vals = product(both, 1, cols), product(both, 2, cols)
                for h in range(2):
                    kb[pl.ds(h * half + begin, block), cols] = keys[h * block : (h + 1) * block]
                    vb[pl.ds(h * half + begin, block), cols] = vals[h * block : (h + 1) * block]
                qb[pl.ds(begin, block), cols] = product(here, 0, cols)

        attend_and_send()

    @pl.when(compute & jnp.logical_not(first))
    def _():
        for step in range(2):
            part = mine if step == 0 else 1 - mine

            @pl.loop(0, pieces)
            def _(k):
                piece_copy(part, k, 0, twin).wait_recv()

            if step == 0:
                ready()
            normalise(part * half, half)
            sl = pl.ds(pl.multiple_of(part * half, half), half)
            for n in range(width // tile):
                cols = pl.ds(n * tile, tile)
                x = nrm[sl, :]
                kb[sl, cols] = product(x, 1, cols)
                vb[sl, cols] = product(x, 2, cols)
                if step == 0:
                    qb[:, cols] = product(x, 0, cols)

        attend_and_send()

    @pl.when(compute)
    def _():
        @pl.when(jnp.logical_not(last))
        def _():
            for k in range(pieces):
                hop_copy(k).wait_send()

        @pl.when(last)
        def _():
            @pl.loop(0, half // 8)
            def _(j):
                @pl.when(jnp.logical_not(fin_is_self(j)))
                def _():
                    fin_copy(j).wait_send()

    @pl.when(first)
    def _():
        @pl.loop(0, nz)
        def _(b):
            for h in range(2):
                @pl.when(b * 4 + h * 2 != lon)
                def _():
                    in_copy(b, h).wait_send()

    dec_copy.wait()
    last_copy.wait()
    pltpu.make_async_copy(outl.at[pl.ds(0, 8)], fin, fin_recv).wait()
    x = fin[...].astype(F32)
    square = jnp.mean(x * x, axis=-1, keepdims=True)
    final = (x * lax.rsqrt(square + EPSILON) * final_gain[...]).astype(BF16)
    out[...] = jnp.dot(final, dec[...], preferred_element_type=F32)


def body(dims, patches, encoder_weight, layer_weights, layer_gains, final_gain, decoder_weight):
    bands, band_rows, own, values = patches.shape
    width = encoder_weight.shape[1]
    out_values = decoder_weight.shape[1]
    segs, lons = dims
    rows = own * lons
    half = rows // 2
    pieces = half // 8
    anyspace = pl.BlockSpec(memory_space=pl.ANY)
    vmem = pl.BlockSpec(memory_space=pltpu.VMEM)
    dma = pltpu.SemaphoreType.DMA
    decoded = pl.pallas_call(
        functools.partial(kernel, dims),
        out_shape=pltpu.VMEM((own, out_values), F32),
        in_specs=[anyspace] * 6,
        out_specs=vmem,
        scratch_shapes=[
            pltpu.VMEM((lons, own, values), BF16),
            pltpu.VMEM((values, width), BF16),
            pltpu.VMEM((4, width, width), BF16),
            pltpu.VMEM((width, out_values), BF16),
            pltpu.VMEM((1, width), F32),
            pltpu.VMEM((1, width), F32),
            pltpu.VMEM((rows, width), BF16),
            pltpu.VMEM((rows, width), BF16),
            pltpu.VMEM((half, width), BF16),
            pltpu.VMEM((rows, width), BF16),
            pltpu.VMEM((rows, width), BF16),
            pltpu.VMEM((half, width), BF16),
            pltpu.VMEM((half, width), BF16),
            pltpu.VMEM((8, width), BF16),
            dma((8,)),
            dma((lons // 2,)),
            dma((lons,)),
            dma((pieces,)),
            dma((2 * pieces,)),
            dma((2 * pieces,)),
            dma((half // 8,)),
            dma,
        ],
        compiler_params=pltpu.CompilerParams(collective_id=0, has_side_effects=True),
        name="forecast",
    )(
        patches.reshape(bands, own, values),
        encoder_weight,
        layer_weights.reshape(4, width, width),
        layer_gains.reshape(1, width),
        final_gain.reshape(1, width),
        decoder_weight,
    )
    return decoded.reshape(1, band_rows, own, out_values)


def solution(mesh):
    dims = (mesh.shape["segment"], mesh.shape["lon"])
    in_specs = (
        P(None, None, "lon", None),
        P(),
        P("segment", None, None, None),
        P("segment", None),
        P(),
        P(),
    )
    out_specs = P("segment", None, "lon", None)
    return jax.shard_map(
        functools.partial(body, dims), mesh=mesh, in_specs=in_specs, out_specs=out_specs, check_vma=False
    )
```

```python
import functools
import math

import jax
import jax.numpy as jnp
from jax import lax
from jax.experimental import pallas as pl
from jax.experimental.pallas import tpu as pltpu
from jax.sharding import PartitionSpec as P

HEAD = 64
SOFTCAP = 5.0
EPSILON = 1e-06
MESH = pl.DeviceIdType.MESH
SPLIT = 64
F32 = jnp.float32
BF16 = jnp.bfloat16


def kernel(
    dims,
    patches,
    encoder_weight,
    layer_weights,
    layer_gain,
    last_gain,
    decoder_weight,
    out,
    pin,
    enc,
    wts,
    dec,
    gain,
    final_gain,
    lat,
    nrm,
    qb,
    kb,
    vb,
    att,
    outl,
    fin,
    w_sem,
    in_send,
    in_recv,
    hop_send,
    hop_recv,
    fwd_send,
    fin_send,
    fin_recv,
):
    segs, lons = dims
    nz = lons // 4
    rows_own = patches.shape[1]
    rows = lat.shape[0]
    width = lat.shape[1]
    half = rows // 2
    split = half * SPLIT // 128 // 16 * 16 or 16
    tile = min(256, width)
    pieces = hop_send.shape[0]
    grain = half // pieces
    s = lax.axis_index("segment")
    lon = lax.axis_index("lon")
    z, xlo, core = lon // 4, lax.rem(lon // 2, 2), lax.rem(lon, 2)
    first, last = s == 0, s == segs - 1
    compute = core == 0
    mine = lax.rem(xlo + s, 2)
    pair = z * 4 + (1 - xlo) * 2
    twin = z * 4 + xlo * 2
    forwarder = jnp.logical_not(compute) & jnp.logical_not(first)

    barrier = pltpu.get_barrier_semaphore()

    def greet(seg, lon_id):
        pl.semaphore_signal(barrier, inc=1, device_id=(seg, lon_id), device_id_type=MESH)

    @pl.when(compute & first)
    def _():
        @pl.loop(0, lons)
        def _(i):
            source = lax.rem(lon + lons // 2 + i, lons)

            @pl.when(source != lon)
            def _():
                greet(0, source)

    @pl.when(compute & jnp.logical_not(first))
    def _():
        greet(s, twin + 1)
        greet(s, pair + 1)

    @pl.when(forwarder)
    def _():
        greet(s - 1, pair)

    fin_lon = s * 4 + xlo * 2
    fin_self = last & (fin_lon == lon)

    @pl.when(jnp.logical_not(fin_self))
    def _():
        greet(segs - 1, fin_lon)

    def w_copy(i):
        return pltpu.make_async_copy(layer_weights.at[i], wts.at[i], w_sem.at[i])

    enc_copy = pltpu.make_async_copy(encoder_weight, enc, w_sem.at[4])
    dec_copy = pltpu.make_async_copy(decoder_weight, dec, w_sem.at[5])
    gain_copy = pltpu.make_async_copy(layer_gain, gain, w_sem.at[6])
    last_copy = pltpu.make_async_copy(last_gain, final_gain, w_sem.at[7])

    @pl.when(compute & first)
    def _():
        enc_copy.start()

    @pl.when(compute)
    def _():
        gain_copy.start()
        for i in range(4):
            w_copy(i).start()

    dec_copy.start()
    last_copy.start()

    def count(flag, number):
        return jnp.where(flag, number, 0)

    targets = (
        count(first, 2 * nz)
        - count(first & compute, 1)
        + count(compute & jnp.logical_not(last), 1)
        + count(forwarder, 2)
        + count(compute & last, 2 * nz)
        - count(compute & fin_self, 1)
    )

    @pl.when(targets > 0)
    def _():
        pl.semaphore_wait(barrier, targets)

    def place(e):
        far = nz // 2
        return jnp.where(e >= far, jnp.maximum(2 * (e - far) - 1, 0), jnp.minimum(2 * (far - e), nz - 1))

    def offset(at):
        return nz // 2 + jnp.where(lax.rem(at, 2) == 1, (at + 1) // 2, -(at // 2))

    def in_slot(b):
        return (1 - xlo) * (2 * nz) + place(lax.rem(z - b + nz, nz)) * 2 + core

    def in_copy(b, h):
        slot = in_slot(b)
        return pltpu.make_async_remote_copy(
            src_ref=patches.at[b],
            dst_ref=pin.at[slot],
            send_sem=in_send.at[b * 2 + h],
            recv_sem=in_recv.at[slot],
            device_id=(0, b * 4 + h * 2),
            device_id_type=MESH,
        )

    def in_local(b):
        slot = in_slot(b)
        return pltpu.make_async_copy(patches.at[b], pin.at[slot], in_recv.at[slot])

    @pl.when(first)
    def _():
        @pl.loop(0, nz)
        def _(d):
            b = lax.rem(z + offset(nz - 1 - d), nz)
            for i in range(2):
                h = 1 - xlo if i == 0 else xlo

                @pl.when(b * 4 + h * 2 != lon)
                def _():
                    in_copy(b, h).start()

        @pl.when(compute)
        def _():
            in_local(z).start()

    def piece_copy(part, k, sem, to):
        chunk = pl.ds(pl.multiple_of(part * half + k * grain, grain), grain)
        return pltpu.make_async_remote_copy(
            src_ref=lat.at[chunk],
            dst_ref=lat.at[chunk],
            send_sem=fwd_send.at[sem],
            recv_sem=hop_recv.at[part * pieces + k],
            device_id=(s, to),
            device_id_type=MESH,
        )

    @pl.when(forwarder)
    def _():
        @pl.loop(0, pieces)
        def _(k):
            piece_copy(mine, k, k, pair).wait_recv()
            piece_copy(mine, k, k, pair).start()
            piece_copy(mine, k, pieces + k, twin).start()

        @pl.loop(0, pieces)
        def _(k):
            piece_copy(mine, k, k, pair).wait_send()
            piece_copy(mine, k, pieces + k, twin).wait_send()

    lane = lax.broadcasted_iota(jnp.int32, (1, 128), 1)
    low = lane < HEAD

    def normalise(base, many):
        for r in range(many // 16):
            sl = pl.ds(pl.multiple_of(base + r * 16, 16), 16)
            x = lat[sl, :].astype(F32)
            square = jnp.mean(x * x, axis=-1, keepdims=True)
            nrm[sl, :] = (x * lax.rsqrt(square + EPSILON) * gain[...]).astype(BF16)

    def product(x, which, cols):
        return jnp.dot(x, wts[which, :, cols], preferred_element_type=F32).astype(BF16)

    def ready():
        gain_copy.wait()
        for i in range(4):
            w_copy(i).wait()

    def hop_copy(k):
        return pltpu.make_async_remote_copy(
            src_ref=outl.at[pl.ds(k * grain, grain)],
            dst_ref=lat.at[pl.ds(pl.multiple_of(mine * half + k * grain, grain), grain)],
            send_sem=hop_send.at[k],
            recv_sem=hop_recv.at[mine * pieces + k],
            device_id=(s + 1, pair + 1),
            device_id_type=MESH,
        )

    def fin_target(j):
        return lax.rem(z + offset(j // 2), nz) * 4 + xlo * 2 + lax.rem(j, 2)

    def fin_is_self(j):
        return (z == s) & (fin_target(j) == lon)

    def fin_copy(j):
        return pltpu.make_async_remote_copy(
            src_ref=outl.at[pl.ds(pl.multiple_of(j * 8, 8), 8)],
            dst_ref=fin,
            send_sem=fin_send.at[j],
            recv_sem=fin_recv,
            device_id=(z, fin_target(j)),
            device_id_type=MESH,
        )

    def attend_and_send():
        for start, qrows in ((0, split), (split, half - split)):
            for hp in range(width // 128):
                lanes = pl.ds(hp * 128, 128)
                q = qb[pl.ds(start, qrows), lanes]
                zero = jnp.zeros_like(q)
                qs = jnp.concatenate([jnp.where(low, q, zero), jnp.where(low, zero, q)], axis=0)
                scores = lax.dot_general(
                    qs, kb[:, lanes], (((1,), (1,)), ((), ())), preferred_element_type=F32
                )
                capped = jnp.tanh(scores * (1.0 / (SOFTCAP * math.sqrt(HEAD))))
                raised = jnp.exp2(capped * (SOFTCAP * math.log2(math.e)))
                total = jnp.sum(raised, axis=-1, keepdims=True)
                mixed = jnp.dot(raised.astype(BF16), vb[:, lanes], preferred_element_type=F32)
                mixed = mixed * (1.0 / total)
                att[pl.ds(0, qrows), lanes] = jnp.where(low, mixed[:qrows], mixed[qrows:]).astype(BF16)

            for n in range(width // tile):
                cols = pl.ds(n * tile, tile)
                y = jnp.dot(att[pl.ds(0, qrows), :], wts[3, :, cols], preferred_element_type=F32)
                before = lat[pl.ds(pl.multiple_of(mine * half + start, 16), qrows), cols]
                outl[pl.ds(start, qrows), cols] = (before.astype(F32) + y).astype(BF16)

            @pl.when(jnp.logical_not(last))
            def _():
                for k in range(start // grain, (start + qrows) // grain):
                    hop_copy(k).start()

            @pl.when(last)
            def _():
                @pl.loop(start // 8, (start + qrows) // 8)
                def _(j):
                    @pl.when(fin_is_self(j))
                    def _():
                        pltpu.make_async_copy(outl.at[pl.ds(pl.multiple_of(j * 8, 8), 8)], fin, fin_recv).start()

                    @pl.when(jnp.logical_not(fin_is_self(j)))
                    def _():
                        fin_copy(j).start()

    @pl.when(compute & first)
    def _():
        enc_copy.wait()
        block = half // 2
        for begin in (block, 0):
            @pl.loop(0, 2 * nz)
            def _(j):
                at = lax.rem(j, nz) + (j // nz) * (2 * nz) + begin // 8
                pltpu.make_async_copy(patches.at[0], pin.at[at], in_recv.at[at]).wait()

            values = pin.shape[2]
            flat = jnp.concatenate(
                [pin[pl.ds((h * half + begin) // 8, nz)].reshape(block, values) for h in range(2)], axis=0
            )
            for n in range(width // tile):
                cols = pl.ds(n * tile, tile)
                fresh = jnp.dot(flat, enc[:, cols], preferred_element_type=F32).astype(BF16)
                lat[pl.ds(begin, block), cols] = fresh[:block]
                lat[pl.ds(half + begin, block), cols] = fresh[block:]

            if begin:
                ready()

            normalise(begin, block)
            normalise(half + begin, block)
            both = jnp.concatenate([nrm[pl.ds(h * half + begin, block), :] for h in range(2)], axis=0)
            here = nrm[pl.ds(pl.multiple_of(mine * half + begin, block), block), :]
            for n in range(width // tile):
                cols = pl.ds(n * tile, tile)
                keys, vals = product(both, 1, cols), product(both, 2, cols)
                for h in range(2):
                    kb[pl.ds(h * half + begin, block), cols] = keys[h * block : (h + 1) * block]
                    vb[pl.ds(h * half + begin, block), cols] = vals[h * block : (h + 1) * block]
                qb[pl.ds(begin, block), cols] = product(here, 0, cols)

        attend_and_send()

    @pl.when(compute & jnp.logical_not(first))
    def _():
        for step in range(2):
            part = mine if step == 0 else 1 - mine

            @pl.loop(0, pieces)
            def _(k):
                piece_copy(part, k, 0, twin).wait_recv()

            if step == 0:
                ready()
            normalise(part * half, half)
            sl = pl.ds(pl.multiple_of(part * half, half), half)
            for n in range(width // tile):
                cols = pl.ds(n * tile, tile)
                x = nrm[sl, :]
                kb[sl, cols] = product(x, 1, cols)
                vb[sl, cols] = product(x, 2, cols)
                if step == 0:
                    qb[:, cols] = product(x, 0, cols)

        attend_and_send()

    @pl.when(compute)
    def _():
        @pl.when(jnp.logical_not(last))
        def _():
            for k in range(pieces):
                hop_copy(k).wait_send()

        @pl.when(last)
        def _():
            @pl.loop(0, half // 8)
            def _(j):
                @pl.when(jnp.logical_not(fin_is_self(j)))
                def _():
                    fin_copy(j).wait_send()

    @pl.when(first)
    def _():
        @pl.loop(0, nz)
        def _(b):
            for h in range(2):
                @pl.when(b * 4 + h * 2 != lon)
                def _():
                    in_copy(b, h).wait_send()

    dec_copy.wait()
    last_copy.wait()
    pltpu.make_async_copy(outl.at[pl.ds(0, 8)], fin, fin_recv).wait()
    x = fin[...].astype(F32)
    square = jnp.mean(x * x, axis=-1, keepdims=True)
    final = (x * lax.rsqrt(square + EPSILON) * final_gain[...]).astype(BF16)
    out[...] = jnp.dot(final, dec[...], preferred_element_type=F32)


def body(dims, patches, encoder_weight, layer_weights, layer_gains, final_gain, decoder_weight):
    bands, band_rows, own, values = patches.shape
    width = encoder_weight.shape[1]
    out_values = decoder_weight.shape[1]
    segs, lons = dims
    rows = own * lons
    half = rows // 2
    pieces = half // 8
    anyspace = pl.BlockSpec(memory_space=pl.ANY)
    vmem = pl.BlockSpec(memory_space=pltpu.VMEM)
    dma = pltpu.SemaphoreType.DMA
    decoded = pl.pallas_call(
        functools.partial(kernel, dims),
        out_shape=pltpu.VMEM((own, out_values), F32),
        in_specs=[anyspace] * 6,
        out_specs=vmem,
        scratch_shapes=[
            pltpu.VMEM((lons, own, values), BF16),
            pltpu.VMEM((values, width), BF16),
            pltpu.VMEM((4, width, width), BF16),
            pltpu.VMEM((width, out_values), BF16),
            pltpu.VMEM((1, width), F32),
            pltpu.VMEM((1, width), F32),
            pltpu.VMEM((rows, width), BF16),
            pltpu.VMEM((rows, width), BF16),
            pltpu.VMEM((half, width), BF16),
            pltpu.VMEM((rows, width), BF16),
            pltpu.VMEM((rows, width), BF16),
            pltpu.VMEM((half, width), BF16),
            pltpu.VMEM((half, width), BF16),
            pltpu.VMEM((8, width), BF16),
            dma((8,)),
            dma((lons // 2,)),
            dma((lons,)),
            dma((pieces,)),
            dma((2 * pieces,)),
            dma((2 * pieces,)),
            dma((half // 8,)),
            dma,
        ],
        compiler_params=pltpu.CompilerParams(collective_id=0, has_side_effects=True),
        name="forecast",
    )(
        patches.reshape(bands, own, values),
        encoder_weight,
        layer_weights.reshape(4, width, width),
        layer_gains.reshape(1, width),
        final_gain.reshape(1, width),
        decoder_weight,
    )
    return decoded.reshape(1, band_rows, own, out_values)


def solution(mesh):
    dims = (mesh.shape["segment"], mesh.shape["lon"])
    in_specs = (
        P(None, None, "lon", None),
        P(),
        P("segment", None, None, None),
        P("segment", None),
        P(),
        P(),
    )
    out_specs = P("segment", None, "lon", None)
    return jax.shard_map(
        functools.partial(body, dims), mesh=mesh, in_specs=in_specs, out_specs=out_specs, check_vma=False
    )
```
